256 devices in a mesh: expert: 128 (over x, z, y), dp: 2 (over core).
Axes of the slice: x: 4, y: 4, z: 8, core: 2. Of those that a mesh axis runs over, the one named last changes fastest.
Arguments:
- pooled: bfloat16 [65536, 256], P(('expert', 'dp')), may hold values from -6 to 6
- routes: int32 [65536, 2], P(('expert', 'dp')), may hold values from 0 to 127, all different within a row; in each aligned block of 256 rows (0 to 255, 256 to 511, ...) at most 6 rows name the same one
- labels: int32 [65536, 2], P(('expert', 'dp')), may hold values from 0 to 1
- in_weight: bfloat16 [128, 4096, 256], P('expert'), may hold values from -0.375 to 0.375
- out_weight: bfloat16 [128, 4096, 256], P('expert'), may hold values from -0.09375 to 0.09375
- gate_weight: bfloat16 [128, 2, 256], replicated, may hold values from -0.375 to 0.375
- tower_weight: float32 [2, 256], replicated, may hold values from -0.375 to 0.375
- tower_bias: float32 [2], replicated, may hold values from -3 to 3
- bag_rows: int32 [131072], P(('expert', 'dp')), may hold values from 0 to 1023
- bag_sample: int32 [131072], P(('expert', 'dp')), may hold values from 0 to 255
- bag_weight: float32 [131072], P(('expert', 'dp')), may hold values from 0.5 to 2
- row_table: float32 [131072, 256], P('expert'), may hold values from -6 to 6
Outputs:
- in_grad: float32 [128, 4096, 256], P('expert', 'dp')
- out_grad: float32 [128, 4096, 256], P('expert', 'dp')
- gate_grad: float32 [128, 2, 256], P('expert')
- tower_grad: float32 [2, 256], replicated
- new_table: float32 [131072, 256], P('expert')
The draws below stay inside these ranges and needn't reach their ends.
Inputs may be any that keep to these rules, and one draw needn't show every extreme that they name: `routes`: within each device's 256 rows no expert is named more than 6 times, a bound that some block reaches; a row's two experts differ.
All inputs are finite; a program needn't handle non-finite values.
Results may differ from the reference program's by a relative error of at most 0.0041.
Values may be sent and summed in bfloat16 or wider, within the bound.
No kernel may reach another device: no remote copies, remote signals or barrier semaphores. Data moves between devices by JAX's collectives and lax.ppermute only.
A program may use at most 128 MiB of HBM per device.

```python
import math
import jax
import jax.numpy as jnp
import numpy as np
from jax import lax

FEAT = 256
HIDDEN_SIZE = 4096
TASKS = 2
TOK_DEV = 256
BAG_DEV = 512
TROWS_DEV = 1024
EXPERTS = 128
CAP = 6
PER_OWNER = 4
TOKENS = 65536
BAG_ALL = 131072
TROWS_ALL = 131072
N_EXPERT = 128
N_DP = 2


def place_ends(values, stream_key, low, top_value):
    index_at = [jax.random.randint(jax.random.fold_in(stream_key, axis), (), 0, length) for axis, length in enumerate(values.shape)]
    widest = values.shape.index(max(values.shape))
    beside = index_at[:widest] + [(index_at[widest] + 1) % values.shape[widest]] + index_at[widest + 1:]
    return values.at[tuple(index_at)].set(low).at[tuple(beside)].set(top_value)


def block_levels(stream_key, dims, split, low, high):
    gain, own = 1.0, jax.random.fold_in(stream_key, 6)
    for position, shards_of in split:
        steps = jnp.exp(jax.random.uniform(jax.random.fold_in(own, position), (shards_of,), jnp.float32, low / len(split), high / len(split)))
        gain = gain * jnp.repeat(steps, dims[position] // shards_of).reshape([-1 if axis == position else 1 for axis in range(len(dims))])
    return gain


def assign_block(rng, own, number, rows, number_of, top, limit, skew):
    order = jax.random.permutation(rng, number_of)
    crowded, ordinary = load_shares(number_of, rows * top, limit, skew, True), load_shares(number_of, rows * top, limit, skew, False)
    places = jnp.arange(number_of)

    def named(tallies, rotation):
        used = int((tallies > 0).sum())
        fixed = max(1, used // 4)
        shifted = fixed + (places - fixed + rotation * (used - fixed)) % max(1, number_of - fixed)
        return jnp.zeros((number_of,), jnp.int32).at[order[jnp.where(places < fixed, places, shifted)]].set(jnp.asarray(tallies, jnp.int32))

    tallies = jnp.where(number % 4 == 0, named(crowded, number // 4), named(ordinary, number - number // 4 - 1))
    mixed = jax.random.permutation(jax.random.fold_in(own, 3), number_of)
    giver, sink = mixed[0:number_of // 2 * 2:2], mixed[1:number_of // 2 * 2:2]
    room = jnp.minimum(tallies[giver] - 1, limit - tallies[sink]) // 2
    room = jnp.where((giver == order[0]) | (sink == order[0]) | (tallies[sink] == 0), 0, jnp.maximum(room, 0))
    shifted = jax.random.randint(jax.random.fold_in(own, 4), (number_of // 2,), 0, 1 << 20) % (room + 1)
    tallies = tallies.at[giver].add(-shifted).at[sink].add(shifted)
    items = jnp.searchsorted(jnp.cumsum(tallies), jnp.arange(rows * top), side="right").astype(jnp.int32)
    listing = items.reshape(top, rows).T
    listing = listing[jax.random.permutation(jax.random.fold_in(own, 1), rows)]
    rotation = jax.random.randint(jax.random.fold_in(own, 2), (rows, 1), 0, top)
    return jnp.take_along_axis(listing, (jnp.arange(top)[None, :] + rotation) % top, axis=1)


def load_shares(count, total, bound, lean, full):
    portions = [(1 << 20) // math.isqrt(grade ** lean) + 1 for grade in range(1, count + 1)]
    largest = bound if full else min(bound, max(-(-total // count), total * portions[0] // sum(portions)))
    least = 1 if total - largest >= count - 1 else 0
    given, spare = [largest] + [least] * (count - 1), total - largest - least * (count - 1)
    while spare > 0:
        candidates = [i for i in range(1, count) if given[i] < largest] or [i for i in range(1, count) if given[i] < bound]
        pool, budget = sum([portions[i] for i in candidates]), spare
        for i in candidates:
            more = min(bound - given[i], max(1, budget * portions[i] // pool), spare)
            given[i] = given[i] + more
            spare = spare - more
    return np.array(given)


def noise(own_key, shape, deviation, most, pieces=(), held_as=jnp.bfloat16):
    array = jax.random.normal(own_key, shape, jnp.float32) * deviation
    if len(pieces) > 0:
        array = block_levels(own_key, shape, pieces, -0.22, 0.18) * array
    return jnp.clip(array, min=-most, max=most).astype(held_as)


def setup_inputs(seed: int = 0) -> dict:
    arg_keys = jax.random.split(jax.random.key(seed), 13)
    pooled = noise(arg_keys[0], (TOKENS, FEAT), 1.0, 6.0, ((0, 256),))
    routes_keys = jax.random.split(jax.random.fold_in(arg_keys[1], 1), TOKENS // TOK_DEV)
    routes_turns = jax.random.permutation(jax.random.fold_in(arg_keys[1], 3), TOKENS // TOK_DEV)
    routes = jax.vmap(lambda own, number: assign_block(jax.random.fold_in(arg_keys[1], 2), own, number, TOK_DEV, EXPERTS, 2, CAP, 2))(routes_keys, routes_turns).reshape((TOKENS, 2))
    labels = place_ends(jax.random.randint(arg_keys[2], (TOKENS, TASKS), 0, 2), jax.random.fold_in(arg_keys[2], 1), 0, 1).astype(jnp.int32)
    in_weight = noise(arg_keys[3], (EXPERTS, HIDDEN_SIZE, FEAT), FEAT ** -0.5, 0.375, ((0, 128),))
    out_weight = noise(arg_keys[4], (EXPERTS, HIDDEN_SIZE, FEAT), HIDDEN_SIZE ** -0.5, 0.09375, ((0, 128),))
    gate_weight = noise(arg_keys[5], (EXPERTS, TASKS, FEAT), FEAT ** -0.5, 0.375)
    tower_weight = noise(arg_keys[6], (TASKS, FEAT), FEAT ** -0.5, 0.375, (), jnp.float32)
    tower_bias = noise(arg_keys[7], (TASKS,), 1.0, 3.0, (), jnp.float32)
    bag_rows = place_ends(jax.random.randint(arg_keys[8], (BAG_ALL,), 0, TROWS_DEV), jax.random.fold_in(arg_keys[8], 1), 0, TROWS_DEV - 1).astype(jnp.int32)
    bag_sample = place_ends(jax.random.randint(arg_keys[9], (BAG_ALL,), 0, TOK_DEV), jax.random.fold_in(arg_keys[9], 1), 0, TOK_DEV - 1).astype(jnp.int32)
    bag_weight = jnp.clip(jnp.exp(math.log(2.0) - 1.3862944 * jax.random.uniform(arg_keys[10], (BAG_ALL,), jnp.float32) ** block_levels(arg_keys[10], (BAG_ALL,), ((0, 256),), -0.2, 0.2)), 0.5, 2.0)
    row_table = noise(arg_keys[11], (TROWS_ALL, FEAT), 1.0, 6.0, ((0, 128),), jnp.float32)
    return {"pooled": pooled, "routes": routes, "labels": labels, "in_weight": in_weight, "out_weight": out_weight, "gate_weight": gate_weight, "tower_weight": tower_weight, "tower_bias": tower_bias, "bag_rows": bag_rows, "bag_sample": bag_sample, "bag_weight": bag_weight, "row_table": row_table}


LOSS_SCALE = 32.0
STEP_SIZE = 0.25
HIGH = lax.Precision.HIGHEST

def silu_grad(pre_silu):
    sigma = jax.nn.sigmoid(pre_silu)
    return sigma * (1.0 + pre_silu * (1.0 - sigma))

def reference(pooled, routes, labels, in_weight, out_weight, gate_weight, tower_weight, tower_bias, bag_rows, bag_sample, bag_weight, row_table):
    device_count = N_EXPERT * N_DP
    flat_routes = routes.reshape(device_count, TOK_DEV * 2)
    one_hot_int = (flat_routes[:, :, None] == jnp.arange(EXPERTS, dtype=jnp.int32)[None, None, :]).astype(jnp.int32)
    ranks = jnp.cumsum(one_hot_int, axis=1) - 1
    slot_of = lax.optimization_barrier(jnp.sum(ranks * one_hot_int, axis=2)).astype(jnp.int32)
    slot_index = (flat_routes * CAP + slot_of).astype(jnp.int32)

    def scatter_rows(values):
        empty = jnp.zeros((device_count, EXPERTS * CAP, FEAT), jnp.bfloat16)
        filled = jax.vmap(lambda buffer, where, rows_in: buffer.at[where].set(rows_in))(empty, slot_index, values)
        return filled.reshape(device_count, EXPERTS, CAP, FEAT).transpose(1, 0, 2, 3).reshape(EXPERTS, device_count * CAP, FEAT)

    def collect_rows(values):
        back = values.reshape(EXPERTS, device_count, CAP, FEAT).transpose(1, 0, 2, 3).reshape(device_count, EXPERTS * CAP, FEAT)
        picked = jax.vmap(lambda buffer, where: buffer[where])(back, slot_index)
        return picked.reshape(TOKENS, 2, FEAT)
    paired = jnp.repeat(pooled.reshape(device_count, TOK_DEV, FEAT), 2, axis=1)
    routed_in = scatter_rows(paired)

    def forward(items):
        inputs, in_matrix, out_matrix = items
        pre_silu = lax.dot_general(inputs, in_matrix, (((1,), (1,)), ((), ())), preferred_element_type=jnp.float32)
        hidden_act = jax.nn.silu(pre_silu).astype(jnp.bfloat16)
        return jnp.dot(hidden_act, out_matrix, preferred_element_type=jnp.float32).astype(jnp.bfloat16)
    expert_rows = lax.map(forward, (routed_in, in_weight, out_weight))
    expert_out = collect_rows(expert_rows).astype(jnp.float32)
    one_hot = (routes[:, :, None] == jnp.arange(EXPERTS, dtype=jnp.int32)[None, None, :]).astype(jnp.float32)
    gate_flat = gate_weight.reshape(EXPERTS * TASKS, FEAT)
    all_logits = lax.dot_general(pooled, gate_flat, (((1,), (1,)), ((), ())), preferred_element_type=jnp.float32).reshape(TOKENS, EXPERTS, TASKS)
    chosen = jnp.einsum('nke,net->ntk', one_hot, all_logits, precision=HIGH)
    gate_first = jax.nn.sigmoid(chosen[:, :, 0] - chosen[:, :, 1])
    gate_second = 1.0 - gate_first
    mixture = gate_first[:, :, None] * expert_out[:, None, 0, :] + gate_second[:, :, None] * expert_out[:, None, 1, :]
    task_logit = lax.optimization_barrier(jnp.sum(mixture * tower_weight[None], axis=2)) + tower_bias[None]
    logit_grad = LOSS_SCALE * (jax.nn.sigmoid(task_logit) - labels.astype(jnp.float32))
    tower_grad = jnp.einsum('nt,ntf->tf', logit_grad, mixture, precision=HIGH)
    mixture_grad = logit_grad[:, :, None] * tower_weight[None]
    routed_grad = jnp.stack([lax.optimization_barrier(jnp.sum(gate_first[:, :, None] * mixture_grad, axis=1)), lax.optimization_barrier(jnp.sum(gate_second[:, :, None] * mixture_grad, axis=1))], axis=1).astype(jnp.bfloat16)
    gate_dot = jnp.einsum('ntf,nkf->ntk', mixture_grad, expert_out, precision=HIGH)
    first_grad = (gate_dot[:, :, 0] - gate_dot[:, :, 1]) * gate_first * gate_second
    select_grad = jnp.stack([first_grad, -first_grad], axis=2)
    mix_table = jnp.einsum('nke,ntk->net', one_hot, select_grad, precision=HIGH).reshape(TOKENS, EXPERTS * TASKS)
    gate_grad = lax.dot_general(mix_table, pooled.astype(jnp.float32), (((0,), (0,)), ((), ())), precision=HIGH).reshape(EXPERTS, TASKS, FEAT)
    gate_input = jnp.dot(mix_table, gate_flat.astype(jnp.float32), precision=HIGH)
    routed_back = scatter_rows(routed_grad.reshape(device_count, TOK_DEV * 2, FEAT))

    def backward(items):
        inputs, grad_rows, in_matrix, out_matrix = items
        pre_silu = lax.dot_general(inputs, in_matrix, (((1,), (1,)), ((), ())), preferred_element_type=jnp.float32)
        hidden_act = jax.nn.silu(pre_silu).astype(jnp.bfloat16)
        hidden_grad = lax.dot_general(grad_rows, out_matrix, (((1,), (1,)), ((), ())), preferred_element_type=jnp.float32)
        pre_grad = (hidden_grad * silu_grad(pre_silu)).astype(jnp.bfloat16)
        in_part = lax.dot_general(pre_grad, inputs, (((0,), (0,)), ((), ())), preferred_element_type=jnp.float32)
        out_part = lax.dot_general(hidden_act, grad_rows, (((0,), (0,)), ((), ())), preferred_element_type=jnp.float32)
        input_grad = jnp.dot(pre_grad, in_matrix, preferred_element_type=jnp.float32).astype(jnp.bfloat16)
        return (in_part, out_part, input_grad)
    in_grad, out_grad, input_rows = lax.map(backward, (routed_in, routed_back, in_weight, out_weight))
    input_grad = collect_rows(input_rows).astype(jnp.float32)
    pooled_grad = gate_input + input_grad[:, 0] + input_grad[:, 1]
    entry = jnp.arange(BAG_ALL, dtype=jnp.int32)
    block_of = entry // BAG_DEV
    owner_of = entry % BAG_DEV // PER_OWNER
    sample_of = (block_of * TOK_DEV + bag_sample).astype(jnp.int32)
    row_grad = (bag_weight[:, None] * pooled_grad[sample_of]).astype(jnp.bfloat16)
    target = (owner_of * TROWS_DEV + bag_rows).astype(jnp.int32)
    row_sums = jax.ops.segment_sum(row_grad.astype(jnp.float32), target, num_segments=TROWS_ALL)
    new_table = row_table - STEP_SIZE * row_sums
    return (in_grad, out_grad, gate_grad, tower_grad, new_table)
```

```python
import functools

import jax
import jax.numpy as jnp
from jax import lax
from jax.experimental import pallas as pl
from jax.experimental.pallas import tpu as pltpu
from jax.sharding import Mesh
from jax.sharding import PartitionSpec as P

EXPERT = ("expert_0", "expert_1", "expert_2")
EXPERT_DP = ("expert_0", "expert_1", "expert_2", "dp")

LOSS_SCALE = 32.0
STEP_SIZE = 0.25
BF = jnp.bfloat16
F32 = jnp.float32

ROWS = 2
BLOCKS = 3
PIECES = 3
SLOT_LANES = 4 * PIECES
ROW_LANES = BLOCKS * SLOT_LANES


def dot(left, right):
    return jnp.dot(left, right, preferred_element_type=F32)


def dot_last(left, right):
    return lax.dot_general(left, right, (((1,), (1,)), ((), ())), preferred_element_type=F32)


def iota(shape, dim):
    return lax.broadcasted_iota(jnp.int32, shape, dim)


def ones_where(mask):
    return jnp.where(mask, 1.0, 0.0).astype(BF)


def three_pieces(value):
    high = value.astype(BF)
    rest = value - high.astype(F32)
    middle = rest.astype(BF)
    low = (rest - middle.astype(F32)).astype(BF)
    return high, middle, low


def tower_pieces(tower):
    pieces = three_pieces(tower)
    row = iota((8, tower.shape[1]), 0)
    stacked = jnp.zeros((8, tower.shape[1]), F32)
    for p, piece in enumerate(pieces):
        for t in range(2):
            stacked = jnp.where(row == 2 * p + t, piece[t : t + 1].astype(F32), stacked)
    return stacked.astype(BF)


def silu_and_slope(pre):
    sigma = 0.5 * jnp.tanh(0.5 * pre) + 0.5
    act = pre * sigma
    return act, sigma + act * (1.0 - sigma)


def full(shape):
    return pl.BlockSpec(shape, lambda *_: (0,) * len(shape))


def call(kernel, out_shape, ins, flops, name, **more):
    return pl.pallas_call(
        kernel,
        out_shape=out_shape,
        cost_estimate=pl.CostEstimate(flops=flops, transcendentals=0, bytes_accessed=1 << 20),
        name=name,
        **more,
    )(*ins)


def dispatch_kernel(routes_t, pooled, out):
    tok = pooled.shape[0]
    shape = (out.shape[0], tok)
    row = iota(shape, 0)
    owner = row >> 1
    named = (owner == routes_t[0:1, :]) | (owner == routes_t[1:2, :])
    earlier = ones_where(iota((tok, tok), 0) < iota((tok, tok), 1))
    rank = dot(ones_where(named), earlier)
    first = (BLOCKS * (row & 1)).astype(F32)
    feature = pooled.shape[1]
    for c in range(BLOCKS):
        pick = ones_where(named & (rank == first + c))
        out[:, c * feature : (c + 1) * feature] = dot(pick, pooled[...]).astype(BF)


def prepare_kernel(
    routes, routes_t, pooled, gate_flat, bag_rows, bag_sample, take, put, gate_rows, gates, side, bag_pick
):
    tok = pooled.shape[0]
    rows = gate_flat.shape[0]
    row = iota((tok, rows), 1)
    named = [(row >> 1) == routes[:, k : k + 1] for k in range(2)]
    earlier = ones_where(iota((tok, tok), 0) > iota((tok, tok), 1))
    rank = dot(earlier, ones_where(named[0] | named[1]))
    first = (BLOCKS * (row & 1)).astype(F32)
    for k in range(2):
        for c in range(BLOCKS):
            take[BLOCKS * k + c] = ones_where(named[k] & (rank == first + c))
    row_t = iota((rows, tok), 0)
    named_t = [(row_t >> 1) == routes_t[k : k + 1, :] for k in range(2)]
    later = ones_where(iota((tok, tok), 0) < iota((tok, tok), 1))
    rank_t = dot(ones_where(named_t[0] | named_t[1]), later)
    first_t = (BLOCKS * (row_t & 1)).astype(F32)
    for k in range(2):
        for c in range(BLOCKS):
            put[BLOCKS * k + c] = ones_where(named_t[k] & (rank_t == first_t + c))
    logits = dot_last(pooled[...], gate_flat[...])
    lane = iota((tok, 128), 1)
    gate = jnp.zeros((tok, 128), F32)
    for t in range(2):
        of_task = (row & 1) == t
        chosen = [
            jnp.sum(jnp.where(named[k] & of_task, logits, 0.0), axis=1, keepdims=True)
            for k in range(2)
        ]
        gate = jnp.where(lane == t, jax.nn.sigmoid(chosen[0] - chosen[1]), gate)
        signs = jnp.where(named[0] & of_task, 1.0, jnp.where(named[1] & of_task, -1.0, 0.0))
        gate_rows[t] = dot(signs.astype(BF), gate_flat[...])
    gates[...] = gate
    numbers = jnp.zeros((rows, 128), jnp.int32)
    side_lane = iota((rows, 128), 1)
    for b in range(2):
        number = bag_rows[:, b : b + 1]
        numbers = jnp.where(side_lane == ROW_LANES + 2 * b, number >> 8, numbers)
        numbers = jnp.where(side_lane == ROW_LANES + 2 * b + 1, number & 255, numbers)
        bag_pick[b] = ones_where(bag_sample[:, b : b + 1] == iota((rows, tok), 1))
    side[...] = numbers.astype(F32)


def expert_kernel(x, w_in, w_out, tower, out, total):
    step = pl.program_id(0)
    rows = x.shape[0]
    feature = w_in.shape[1]
    wide = 3 * feature

    @pl.when(step == 0)
    def _():
        total[...] = jnp.zeros_like(total)

    slopes = dot_last(tower_pieces(tower[...]), w_out[...])
    slope = [slopes[t : t + 1] + slopes[2 + t : 3 + t] + slopes[4 + t : 5 + t] for t in range(2)]
    for c in range(BLOCKS):
        pre = dot_last(x[:, c * feature : (c + 1) * feature], w_in[...])
        act, grad = silu_and_slope(pre)
        at = c * wide
        total[:, at : at + feature] += dot(act.astype(BF), w_out[...])
        for t in range(2):
            cols = slice(at + (1 + t) * feature, at + (2 + t) * feature)
            total[:, cols] += dot((grad * slope[t]).astype(BF), w_in[...])

    @pl.when(step == pl.num_programs(0) - 1)
    def _():
        out[...] = total[...].astype(BF)


def half_kernel(half, x, x_other, w_in, w_out, tower, act_t, grad_t, slope):
    del half
    feature = w_in.shape[1]
    rows = x.shape[0]
    slopes = dot_last(w_out[...], tower_pieces(tower[...]))
    lane = iota(slope.shape, 1)
    wide = jnp.zeros(slope.shape, F32)
    for t in range(2):
        column = slopes[:, t : t + 1] + slopes[:, 2 + t : 3 + t] + slopes[:, 4 + t : 5 + t]
        wide = jnp.where(lane == t, column, wide)
    slope[...] = wide
    for r, source in enumerate((x, x_other)):
        for c in range(BLOCKS):
            pre = dot_last(w_in[...], source[:, c * feature : (c + 1) * feature])
            act, grad = silu_and_slope(pre)
            at = (BLOCKS * r + c) * rows
            act_t[:, at : at + rows] = act.astype(BF)
            grad_t[:, at : at + rows] = grad.astype(BF)


def sample_kernel(
    back, take, put, gate_rows, gates, side, bag_pick, labels, tower, bias, bag_weight, out
):
    feature = tower.shape[1]
    wide = 3 * feature
    parts = []
    for k in range(2):
        part = dot(take[BLOCKS * k], back[:, :wide])
        for c in range(1, BLOCKS):
            part += dot(take[BLOCKS * k + c], back[:, c * wide : (c + 1) * wide])
        parts.append(part)
    result = [part[:, :feature] for part in parts]
    gate, towers, first_grad = [], [], []
    pulls = [[None, None], [None, None]]
    for t in range(2):
        weight = tower[t : t + 1, :]
        along = [jnp.sum(result[k] * weight, axis=1, keepdims=True) for k in range(2)]
        first = gates[:, t : t + 1]
        second = 1.0 - first
        logit = first * along[0] + second * along[1] + bias[t]
        label = labels[:, t : t + 1].astype(F32)
        logit_grad = LOSS_SCALE * (jax.nn.sigmoid(logit) - label)
        pulls[0][t], pulls[1][t] = first * logit_grad, second * logit_grad
        first_grad.append(logit_grad * (along[0] - along[1]) * first * second)
        mixture = first * result[0] + second * result[1]
        towers.append(jnp.sum(logit_grad * mixture, axis=0, keepdims=True))
    pooled_grad = first_grad[0] * gate_rows[0] + first_grad[1] * gate_rows[1]
    for k in range(2):
        for t in range(2):
            pooled_grad += pulls[k][t] * parts[k][:, (1 + t) * feature : (2 + t) * feature]
    pieces = three_pieces(pooled_grad)
    for b in range(2):
        picked = sum(dot(bag_pick[b], piece) for piece in pieces)
        out[:, b * feature : (b + 1) * feature] = (bag_weight[:, b : b + 1] * picked).astype(BF)
    tok = gates.shape[0]
    lane = iota((tok, 128), 1)
    blocks = [None] * BLOCKS
    for k in range(2):
        sign = 1.0 if k == 0 else -1.0
        values = [pulls[k][0], pulls[k][1], sign * first_grad[0], sign * first_grad[1]]
        packed = jnp.zeros((tok, 128), F32)
        for v, value in enumerate(values):
            for p, piece in enumerate(three_pieces(value)):
                packed = jnp.where(lane == PIECES * v + p, piece.astype(F32), packed)
        packed = packed.astype(BF)
        for c in range(BLOCKS):
            placed = dot(put[BLOCKS * k + c], packed)
            blocks[c] = placed if blocks[c] is None else blocks[c] + placed
    extra = side[...] + blocks[0]
    for c in range(1, BLOCKS):
        extra += pltpu.roll(blocks[c], c * SLOT_LANES, 1)
    at = 2 * feature
    out[:, at : at + 128] = extra.astype(BF)
    task = iota((out.shape[0], feature), 0) & 1
    total = jnp.where(task == 0, towers[0], towers[1])
    high = total.astype(BF)
    at += 128
    out[:, at : at + feature] = high
    out[:, at + feature : at + 2 * feature] = (total - high.astype(F32)).astype(BF)


def final_kernel(
    x,
    x_other,
    got,
    got_other,
    act_t,
    grad_t,
    slope,
    tower,
    table,
    in_grad,
    out_grad,
    gate_grad,
    tower_grad,
    new_table,
    scaled,
    pulls,
    targets,
):
    feature = tower.shape[1]
    rows = x.shape[0]
    at_side = 2 * feature
    at_tower = at_side + 128
    step = pl.program_id(0)

    @pl.when(step == 0)
    def _():
        gate_total = [jnp.zeros((1, feature), F32) for _ in range(2)]
        tower_total = [jnp.zeros((1, feature), F32) for _ in range(2)]
        lane = iota((rows, 128), 1)
        task = iota((rows, feature), 0) & 1
        wanted = iota((8, 128), 1)
        asked = iota((8, 128), 0)
        select = jnp.zeros((8, 128), F32)
        for b in range(2):
            select = jnp.where((asked == b) & (wanted == ROW_LANES + 2 * b), 256.0, select)
            select = jnp.where((asked == b) & (wanted == ROW_LANES + 2 * b + 1), 1.0, select)
        for r, (inputs, source) in enumerate(((x, got), (x_other, got_other))):
            side = source[:, at_side : at_side + 128]
            targets[8 * r : 8 * r + 8, :] = dot_last(select.astype(BF), side)
            side = side.astype(F32)
            for c in range(BLOCKS):
                values = []
                packed = jnp.zeros((rows, 128), F32)
                for v in range(4):
                    start = c * SLOT_LANES + PIECES * v
                    pieces = [side[:, start + p : start + p + 1] for p in range(PIECES)]
                    values.append(pieces[0] + pieces[1] + pieces[2])
                    if v < 2:
                        for p, piece in enumerate(pieces):
                            packed = jnp.where(lane == PIECES * v + p, piece, packed)
                at = (BLOCKS * r + c) * rows
                pulls[at : at + rows, :] = packed.astype(BF)
                block = inputs[:, c * feature : (c + 1) * feature].astype(F32)
                for t in range(2):
                    cols = slice(t * feature, (t + 1) * feature)
                    scaled[at : at + rows, cols] = (values[t] * block).astype(BF)
                    gate_total[t] += jnp.sum(values[2 + t] * block, axis=0, keepdims=True)
            sent = source[:, at_tower : at_tower + feature].astype(F32)
            sent += source[:, at_tower + feature : at_tower + 2 * feature].astype(F32)
            for t in range(2):
                tower_total[t] += jnp.sum(jnp.where(task == t, sent, 0.0), axis=0, keepdims=True)
        for t in range(2):
            gate_grad[t : t + 1, :] = gate_total[t]
            tower_grad[t : t + 1, :] = tower_total[t]

    both = dot(grad_t[...], scaled[...])
    in_grad[...] = slope[:, 0:1] * both[:, :feature] + slope[:, 1:2] * both[:, feature:]
    along = dot(act_t[...], pulls[...])
    reach = [along[:, 3 * t : 3 * t + 1] + along[:, 3 * t + 1 : 3 * t + 2] + along[:, 3 * t + 2 : 3 * t + 3] for t in range(2)]
    out_grad[...] = reach[0] * tower[0:1, :] + reach[1] * tower[1:2, :]
    depth = table.shape[0]
    number = (step * depth + iota((depth, rows), 0)).astype(F32)
    sums = jnp.zeros(table.shape, F32)
    for r, source in enumerate((got, got_other)):
        for b in range(2):
            hit = ones_where(number == targets[8 * r + b : 8 * r + b + 1, :])
            sums += dot(hit, source[:, b * feature : (b + 1) * feature])
    new_table[...] = table[...] - STEP_SIZE * sums


def exchanged(rows):
    width = rows.shape[1]
    moved = lax.all_to_all(rows.reshape(-1, ROWS, width), EXPERT, split_axis=0, concat_axis=0, tiled=True)
    return moved.reshape(-1, width)


def swapped(shard):
    return lax.ppermute(shard, "dp", [(0, 1), (1, 0)])


def shapes(*items):
    return tuple(jax.ShapeDtypeStruct(shape, dtype) for shape, dtype in items)


def on_device(
    pooled,
    routes,
    labels,
    in_weight,
    out_weight,
    gate_weight,
    tower_weight,
    tower_bias,
    bag_rows,
    bag_sample,
    bag_weight,
    row_table,
):
    owners = lax.axis_size(EXPERT)
    tok, feature = pooled.shape
    hidden = in_weight.shape[1]
    half = hidden // lax.axis_size("dp")
    rows = ROWS * owners
    slots = 2 * BLOCKS * rows
    in_matrix, out_matrix = in_weight[0], out_weight[0]
    gate_flat = gate_weight.reshape(-1, feature)
    routes_t = routes.T
    vmem = pltpu.CompilerParams(vmem_limit_bytes=56 << 20)

    outbound = call(
        dispatch_kernel,
        jax.ShapeDtypeStruct((rows, BLOCKS * feature), BF),
        (routes_t, pooled),
        1 << 27,
        "dispatch",
    )
    received = exchanged(outbound)
    take, put, gate_rows, gates, side, bag_pick = call(
        prepare_kernel,
        shapes(
            ((2 * BLOCKS, tok, rows), BF),
            ((2 * BLOCKS, rows, tok), BF),
            ((2, tok, feature), F32),
            ((tok, 128), F32),
            ((rows, 128), F32),
            ((2, rows, tok), BF),
        ),
        (routes, routes_t, pooled, gate_flat, bag_rows.reshape(rows, 2), bag_sample.reshape(rows, 2)),
        1 << 31,
        "prepare",
    )
    depth = hidden // 4
    message = call(
        expert_kernel,
        jax.ShapeDtypeStruct((rows, 3 * BLOCKS * feature), BF),
        (received, in_matrix, out_matrix, tower_weight),
        7 << 30,
        "expert",
        grid=(hidden // depth,),
        in_specs=[
            full(received.shape),
            pl.BlockSpec((depth, feature), lambda i: (i, 0)),
            pl.BlockSpec((depth, feature), lambda i: (i, 0)),
            full(tower_weight.shape),
        ],
        out_specs=full((rows, 3 * BLOCKS * feature)),
        scratch_shapes=[pltpu.VMEM((rows, 3 * BLOCKS * feature), F32)],
        compiler_params=vmem,
    )
    returned = exchanged(message)
    received_other = swapped(received)
    tile = 256
    tiles = half // tile
    which = jnp.full((1,), lax.axis_index("dp"), jnp.int32)
    act_t, grad_t, slope = call(
        half_kernel,
        shapes(((half, slots), BF), ((half, slots), BF), ((half, 128), F32)),
        (which, received, received_other, in_matrix, out_matrix, tower_weight),
        7 << 30,
        "half",
        grid_spec=pltpu.PrefetchScalarGridSpec(
            num_scalar_prefetch=1,
            grid=(tiles,),
            in_specs=[
                full(received.shape),
                full(received.shape),
                pl.BlockSpec((tile, feature), lambda i, part: (part[0] * tiles + i, 0)),
                pl.BlockSpec((tile, feature), lambda i, part: (part[0] * tiles + i, 0)),
                full(tower_weight.shape),
            ],
            out_specs=[
                pl.BlockSpec((tile, slots), lambda i, part: (i, 0)),
                pl.BlockSpec((tile, slots), lambda i, part: (i, 0)),
                pl.BlockSpec((tile, 128), lambda i, part: (i, 0)),
            ],
        ),
        compiler_params=vmem,
    )
    width = 4 * feature + 128
    sent = call(
        sample_kernel,
        jax.ShapeDtypeStruct((rows, width), BF),
        (
            returned,
            take,
            put,
            gate_rows,
            gates,
            side,
            bag_pick,
            labels,
            tower_weight,
            tower_bias,
            bag_weight.reshape(rows, 2),
        ),
        1 << 29,
        "sample",
        in_specs=[pl.BlockSpec(memory_space=pltpu.VMEM)] * 9
        + [pl.BlockSpec(memory_space=pltpu.SMEM), pl.BlockSpec(memory_space=pltpu.VMEM)],
        compiler_params=vmem,
    )
    got = exchanged(sent)
    got_other = swapped(got)
    table_tile = row_table.shape[0] // tiles
    in_grad, out_grad, gate_grad, tower_grad, new_table = call(
        final_kernel,
        shapes(
            ((half, feature), F32),
            ((half, feature), F32),
            ((2, feature), F32),
            ((2, feature), F32),
            (row_table.shape, F32),
        ),
        (received, received_other, got, got_other, act_t, grad_t, slope, tower_weight, row_table),
        6 << 30,
        "final",
        grid=(tiles,),
        in_specs=[
            full(received.shape),
            full(received.shape),
            full(got.shape),
            full(got.shape),
            pl.BlockSpec((tile, slots), lambda i: (i, 0)),
            pl.BlockSpec((tile, slots), lambda i: (i, 0)),
            pl.BlockSpec((tile, 128), lambda i: (i, 0)),
            full(tower_weight.shape),
            pl.BlockSpec((table_tile, feature), lambda i: (i, 0)),
        ],
        out_specs=[
            pl.BlockSpec((tile, feature), lambda i: (i, 0)),
            pl.BlockSpec((tile, feature), lambda i: (i, 0)),
            full((2, feature)),
            full((2, feature)),
            pl.BlockSpec((table_tile, feature), lambda i: (i, 0)),
        ],
        scratch_shapes=[
            pltpu.VMEM((slots, 2 * feature), BF),
            pltpu.VMEM((slots, 128), BF),
            pltpu.VMEM((16, rows), F32),
        ],
        compiler_params=vmem,
    )
    return (in_grad[None], out_grad[None], gate_grad[None], tower_grad, new_table)


def solution(mesh):
    split = Mesh(
        mesh.devices.reshape(4, 8, 4, mesh.shape["dp"]), ("expert_0", "expert_1", "expert_2", "dp")
    )
    in_specs = (
        P(EXPERT_DP, None),
        P(EXPERT_DP, None),
        P(EXPERT_DP, None),
        P(EXPERT, None, None),
        P(EXPERT, None, None),
        P(),
        P(),
        P(),
        P(EXPERT_DP),
        P(EXPERT_DP),
        P(EXPERT_DP),
        P(EXPERT, None),
    )
    out_specs = (
        P(EXPERT, "dp", None),
        P(EXPERT, "dp", None),
        P(EXPERT, None, None),
        P(),
        P(EXPERT, None),
    )
    return jax.shard_map(
        on_device, mesh=split, in_specs=in_specs, out_specs=out_specs, check_vma=False
    )
```

```python
import functools

import jax
import jax.numpy as jnp
from jax import lax
from jax.experimental import pallas as pl
from jax.experimental.pallas import tpu as pltpu
from jax.sharding import Mesh
from jax.sharding import PartitionSpec as P

EXPERT = ("expert_0", "expert_1", "expert_2")
EXPERT_DP = ("expert_0", "expert_1", "expert_2", "dp")

LOSS_SCALE = 32.0
STEP_SIZE = 0.25
BF = jnp.bfloat16
F32 = jnp.float32
CHUNK = 2048

ROWS = 2
BLOCKS = 3
PIECES = 3
SLOT_LANES = 4 * PIECES
SLOTS = ROWS * BLOCKS
ROW_LANES = SLOTS * SLOT_LANES
ENTRIES = 4
SIDE_ROW = 4
TOWER_ROW = 5


def dot(left, right):
    return jnp.dot(left, right, preferred_element_type=F32)


def dot_last(left, right):
    return lax.dot_general(left, right, (((1,), (1,)), ((), ())), preferred_element_type=F32)


def iota(shape, dim):
    return lax.broadcasted_iota(jnp.int32, shape, dim)


def ones_where(mask):
    return jnp.where(mask, 1.0, 0.0).astype(BF)


def three_pieces(value):
    high = value.astype(BF)
    rest = value - high.astype(F32)
    middle = rest.astype(BF)
    low = (rest - middle.astype(F32)).astype(BF)
    return high, middle, low


def tower_pieces(tower):
    pieces = three_pieces(tower)
    row = iota((8, tower.shape[1]), 0)
    stacked = jnp.zeros((8, tower.shape[1]), F32)
    for p, piece in enumerate(pieces):
        for t in range(2):
            stacked = jnp.where(row == 2 * p + t, piece[t : t + 1].astype(F32), stacked)
    return stacked.astype(BF)


def silu_and_slope(pre):
    sigma = 0.5 * jnp.tanh(0.5 * pre) + 0.5
    act = pre * sigma
    return act, sigma + act * (1.0 - sigma)


def full(shape):
    return pl.BlockSpec(shape, lambda *_: (0,) * len(shape))


def call(kernel, out_shape, ins, flops, name, mib, **more):
    return pl.pallas_call(
        kernel,
        out_shape=out_shape,
        cost_estimate=pl.CostEstimate(flops=flops, transcendentals=0, bytes_accessed=1 << 20),
        name=name,
        compiler_params=pltpu.CompilerParams(vmem_limit_bytes=mib << 20),
        **more,
    )(*ins)


def dispatch_kernel(routes_far, pooled_far, out, routes_t, pooled, sems):
    pairs = ((routes_far, routes_t), (pooled_far, pooled))
    copies = [pltpu.make_async_copy(far, near, sems.at[m]) for m, (far, near) in enumerate(pairs)]
    for copy in copies:
        copy.start()
    tok = pooled.shape[0]
    copies[0].wait()
    shape = (out.shape[0], tok)
    row = iota(shape, 0)
    owner = row >> 1
    named = (owner == routes_t[0:1, :]) | (owner == routes_t[1:2, :])
    earlier = ones_where(iota((tok, tok), 0) < iota((tok, tok), 1))
    rank = dot(ones_where(named), earlier)
    first = (BLOCKS * (row & 1)).astype(F32)
    feature = pooled.shape[1]
    copies[1].wait()
    for c in range(BLOCKS):
        pick = ones_where(named & (rank == first + c))
        out[:, c * feature : (c + 1) * feature] = dot(pick, pooled[...]).astype(BF)


def prepare_kernel(
    routes, routes_t, pooled, gate_flat, labels, bag_rows, bag_sample, bag_weight,
    take, put, gate_rows, lanes, side, bag_pick, bag_scale,
):
    tok = pooled.shape[0]
    rows = gate_flat.shape[0]
    owners = bag_rows.shape[0]
    row = iota((tok, rows), 1)
    named = [(row >> 1) == routes[:, k : k + 1] for k in range(2)]
    earlier = ones_where(iota((tok, tok), 0) > iota((tok, tok), 1))
    rank = dot(earlier, ones_where(named[0] | named[1]))
    first = (BLOCKS * (row & 1)).astype(F32)
    for k in range(2):
        for c in range(BLOCKS):
            take[BLOCKS * k + c] = ones_where(named[k] & (rank == first + c))
    owner = iota((owners, tok), 0)
    named_t = [owner == routes_t[k : k + 1, :] for k in range(2)]
    later = ones_where(iota((tok, tok), 0) < iota((tok, tok), 1))
    rank_t = dot(ones_where(named_t[0] | named_t[1]), later)
    for k in range(2):
        for j in range(SLOTS):
            put[SLOTS * k + j] = ones_where(named_t[k] & (rank_t == float(j)))
    logits = dot_last(pooled[...], gate_flat[...])
    lane = iota((tok, 128), 1)
    gate = jnp.zeros((tok, 128), F32)
    label = jnp.zeros((tok, 128), F32)
    for t in range(2):
        of_task = (row & 1) == t
        chosen = [
            jnp.sum(jnp.where(named[k] & of_task, logits, 0.0), axis=1, keepdims=True)
            for k in range(2)
        ]
        gate = jnp.where(lane == t, jax.nn.sigmoid(chosen[0] - chosen[1]), gate)
        label = jnp.where(lane == t, labels[:, t : t + 1].astype(F32), label)
        signs = jnp.where(named[0] & of_task, 1.0, jnp.where(named[1] & of_task, -1.0, 0.0))
        gate_rows[t] = dot(signs.astype(BF), gate_flat[...])
    lanes[0] = gate
    lanes[1] = label
    numbers = jnp.zeros((owners, 128), jnp.int32)
    side_lane = iota((owners, 128), 1)
    for r in range(ENTRIES):
        number = bag_rows[:, r : r + 1]
        numbers = jnp.where(side_lane == ROW_LANES + 2 * r, number >> 8, numbers)
        numbers = jnp.where(side_lane == ROW_LANES + 2 * r + 1, number & 255, numbers)
    side[...] = numbers.astype(F32)
    tall = bag_pick.shape[0]
    spread = ones_where((iota((tall, owners), 0) >> 3) == iota((tall, owners), 1))
    entry = iota((tall, ENTRIES), 0) & 7
    mine = entry == iota((tall, ENTRIES), 1)

    def column(value):
        spread_out = sum(dot(spread, piece) for piece in three_pieces(value))
        return jnp.sum(jnp.where(mine, spread_out, 0.0), axis=1, keepdims=True)

    sample = column(bag_sample[...].astype(F32))
    tall_iota = iota((tall, tok), 0) & 7
    hit = (sample == iota((tall, tok), 1).astype(F32)) & (tall_iota < ENTRIES)
    bag_pick[...] = ones_where(hit)
    bag_scale[...] = jnp.broadcast_to(column(bag_weight[...]), bag_scale.shape)


def slope_kernel(w_out, tower, slopes):
    found = dot_last(tower_pieces(tower[...]), w_out[...])
    for t in range(2):
        slopes[t : t + 1, :] = found[t : t + 1] + found[2 + t : 3 + t] + found[4 + t : 5 + t]


def expert_kernel(x, w_in, w_out_far, slopes, after, out, total, stacked, w_out, sems):
    del after
    rows = x.shape[0]
    hidden, feature = w_out.shape
    wide = 3 * feature
    units = [slice(at, at + CHUNK) for at in range(0, hidden, CHUNK)]
    arrived = []
    for n, unit in enumerate(units):
        copy = pltpu.make_async_copy(w_out_far.at[unit, :], w_out.at[unit, :], sems.at[n])
        copy.start()
        arrived.append(copy)
    for c in range(BLOCKS):
        stacked[c * rows : (c + 1) * rows, :] = x[:, c * feature : (c + 1) * feature]
    for n, unit in enumerate(units):
        act, grad = silu_and_slope(dot_last(stacked[...], w_in[unit, :]))
        parts = [
            dot((grad * slopes[t : t + 1, unit]).astype(BF), w_in[unit, :]) for t in range(2)
        ]
        act = act.astype(BF)
        arrived[n].wait()
        parts = [dot(act, w_out[unit, :])] + parts
        for p, part in enumerate(parts):
            cols = slice(p * feature, (p + 1) * feature)
            if n == 0:
                total[:, cols] = part
            else:
                total[:, cols] += part
    for c in range(BLOCKS):
        out[:, c * wide : (c + 1) * wide] = total[c * rows : (c + 1) * rows, :].astype(BF)


def half_kernel(half, x, x_other, w_in, w_out, tower, act_t, grad_t, slope):
    del half
    feature = w_in.shape[1]
    rows = x.shape[0]
    slopes = dot_last(w_out[...], tower_pieces(tower[...]))
    lane = iota(slope.shape, 1)
    wide = jnp.zeros(slope.shape, F32)
    for t in range(2):
        column = slopes[:, t : t + 1] + slopes[:, 2 + t : 3 + t] + slopes[:, 4 + t : 5 + t]
        wide = jnp.where(lane == t, column, wide)
    slope[...] = wide
    for r, source in enumerate((x, x_other)):
        for c in range(BLOCKS):
            pre = dot_last(w_in[...], source[:, c * feature : (c + 1) * feature])
            act, grad = silu_and_slope(pre)
            at = (BLOCKS * r + c) * rows
            act_t[:, at : at + rows] = act.astype(BF)
            grad_t[:, at : at + rows] = grad.astype(BF)


def sample_kernel(
    back, take, put_far, gate_rows_far, lanes_far, side_far, bag_pick_far, bag_scale_far,
    tower, bias, after,
    out, put, gate_rows, lanes, side, bag_pick, bag_scale, sems,
):
    del after
    pairs = (
        (lanes_far, lanes),
        (gate_rows_far, gate_rows),
        (bag_pick_far, bag_pick),
        (bag_scale_far, bag_scale),
        (put_far, put),
        (side_far, side),
    )
    copies = [pltpu.make_async_copy(far, near, sems.at[m]) for m, (far, near) in enumerate(pairs)]
    for copy in copies:
        copy.start()
    feature = tower.shape[1]
    wide = 3 * feature
    parts = []
    for k in range(2):
        part = dot(take[BLOCKS * k], back[:, :wide])
        for c in range(1, BLOCKS):
            part += dot(take[BLOCKS * k + c], back[:, c * wide : (c + 1) * wide])
        parts.append(part)
    task_row = iota((128, feature), 0)
    weights = [
        jnp.where(task_row == 0, piece[0:1].astype(F32), jnp.where(task_row == 1, piece[1:2].astype(F32), 0.0)).astype(BF)
        for piece in three_pieces(tower[...])
    ]
    along = []
    for k in range(2):
        result = parts[k][:, :feature].astype(BF)
        along.append(sum(dot_last(result, weight) for weight in weights))
    for copy in copies:
        copy.wait()
    first, label = lanes[0], lanes[1]
    second = 1.0 - first
    lane = iota(first.shape, 1)
    lane_bias = jnp.where(lane == 0, bias[0], bias[1])
    logit = first * along[0] + second * along[1] + lane_bias
    logit_grad = jnp.where(lane < 2, LOSS_SCALE * (jax.nn.sigmoid(logit) - label), 0.0)
    pulls = [first * logit_grad, second * logit_grad]
    first_grad = logit_grad * (along[0] - along[1]) * first * second
    pooled_grad = first_grad[:, 0:1] * gate_rows[0] + first_grad[:, 1:2] * gate_rows[1]
    towers = [0.0, 0.0]
    for k in range(2):
        for t in range(2):
            pull = jnp.broadcast_to(pulls[k][:, t : t + 1], (first.shape[0], feature))
            pooled_grad += pull * parts[k][:, (1 + t) * feature : (2 + t) * feature]
            towers[t] += jnp.sum(pull * parts[k][:, :feature], axis=0, keepdims=True)
    picked = sum(dot(bag_pick[...], piece) for piece in three_pieces(pooled_grad))
    placed = [None] * SLOTS
    for k in range(2):
        signed = first_grad if k == 0 else -first_grad
        packed = 0.0
        for kind, value in enumerate((pulls[k], signed)):
            for p, piece in enumerate(three_pieces(value)):
                piece = piece.astype(F32)
                shift = 2 * PIECES * kind + 2 * p
                packed += pltpu.roll(piece, shift, 1) if shift else piece
        packed = packed.astype(BF)
        for j in range(SLOTS):
            part = dot(put[SLOTS * k + j], packed)
            placed[j] = part if k == 0 else placed[j] + part
    extra = side[...] + placed[0]
    for j in range(1, SLOTS):
        extra += pltpu.roll(placed[j], j * SLOT_LANES, 1)
    tall, owners = bag_pick.shape[0], side.shape[0]
    spread = ones_where(iota((tall, owners), 0) == 8 * iota((tall, owners), 1) + SIDE_ROW)
    extra = dot(spread, extra.astype(BF))
    which = iota((tall, 128), 0) & 7
    for at in range(0, feature, 128):
        cols = slice(at, at + 128)
        value = bag_scale[...] * picked[:, cols]
        for t in range(2):
            value = jnp.where(which == TOWER_ROW + t, towers[t][:, cols], value)
        out[:, cols] = (value + extra if at == 0 else value).astype(BF)


def final_kernel(
    x,
    x_other,
    got,
    got_other,
    act_far,
    grad_far,
    slope,
    tower,
    table,
    in_grad,
    out_grad,
    gate_grad,
    tower_grad,
    new_table,
    scaled,
    routed,
    targets,
    act_t,
    grad_t,
    sems,
):
    feature = tower.shape[1]
    rows = x.shape[0]
    tall = got.shape[0]
    step = pl.program_id(0)
    tile = in_grad.shape[0]

    def arriving(n):
        part = pl.ds(n * tile, tile)
        pairs = ((grad_far, grad_t), (act_far, act_t))
        return [
            pltpu.make_async_copy(far.at[part, :], near.at[part, :], sems.at[m, n])
            for m, (far, near) in enumerate(pairs)
        ]

    @pl.when(step == 0)
    def _():
        for n in range(act_t.shape[0] // tile):
            for copy in arriving(n):
                copy.start()
        gate_total = [jnp.zeros((1, feature), F32) for _ in range(2)]
        tower_total = jnp.zeros((8, feature), F32)
        row = iota((rows, tall), 0)
        expand = ones_where(iota((rows, tall), 1) == 8 * (row >> 1) + SIDE_ROW)
        lane = iota((rows, 128), 1)
        half_lanes = BLOCKS * SLOT_LANES
        odd = (iota((rows, 128), 0) & 1) == 1
        own = (odd & (lane >= half_lanes) & (lane < ROW_LANES)) | (~odd & (lane < half_lanes))
        source_lane = iota((128, feature), 0)
        within = jnp.where(source_lane >= half_lanes, source_lane - half_lanes, source_lane)
        gather = {}
        for c in range(BLOCKS):
            for v in range(4):
                base = c * SLOT_LANES + 2 * PIECES * (v // 2) + v % 2
                gather[c, v] = ones_where((within == base) | (within == base + 2) | (within == base + 4))
        wanted, asked = iota((8, 128), 1), iota((8, 128), 0)
        select = jnp.where(wanted == ROW_LANES + 2 * asked, 256.0, 0.0)
        select = jnp.where(wanted == ROW_LANES + 2 * asked + 1, 1.0, select).astype(BF)
        which = iota((1, tall), 1) & 7
        tower_pick = ones_where((iota((8, tall), 1) & 7) == TOWER_ROW + iota((8, tall), 0))
        for r, (inputs, source) in enumerate(((x, got), (x_other, got_other))):
            numbers = dot_last(select, source[:, :128])
            target = jnp.full((1, tall), -1.0, F32)
            for e in range(ENTRIES):
                moved = pltpu.roll(numbers, tall + e - SIDE_ROW if e < SIDE_ROW else 0, 1)
                target = jnp.where(which == e, moved[e : e + 1], target)
            targets[8 * r : 8 * r + 8, :] = jnp.broadcast_to(target, (8, tall))
            tower_total += dot(tower_pick, source[...])
            side = jnp.where(own, dot(expand, source[:, :128]), 0.0).astype(BF)
            for c in range(BLOCKS):
                values = [dot(side, gather[c, v]) for v in range(4)]
                at = (BLOCKS * r + c) * rows
                block = inputs[:, c * feature : (c + 1) * feature].astype(F32)
                routed[at : at + rows, :] = (
                    values[0] * tower[0:1, :] + values[1] * tower[1:2, :]
                ).astype(BF)
                for t in range(2):
                    cols = slice(t * feature, (t + 1) * feature)
                    scaled[at : at + rows, cols] = (values[t] * block).astype(BF)
                    gate_total[t] += jnp.sum(values[2 + t] * block, axis=0, keepdims=True)
        for t in range(2):
            gate_grad[t : t + 1, :] = gate_total[t]
            tower_grad[t : t + 1, :] = tower_total[t : t + 1]

    for copy in arriving(step):
        copy.wait()
    part = pl.ds(pl.multiple_of(step * tile, tile), tile)
    both = dot(grad_t[part, :], scaled[...])
    in_grad[...] = slope[:, 0:1] * both[:, :feature] + slope[:, 1:2] * both[:, feature:]
    out_grad[...] = dot(act_t[part, :], routed[...])
    depth = table.shape[0]
    number = (step * depth + iota((depth, tall), 0)).astype(F32)
    sums = jnp.zeros(table.shape, F32)
    for r, source in enumerate((got, got_other)):
        sums += dot(ones_where(number == targets[8 * r : 8 * r + 1, :]), source[...])
    new_table[...] = table[...] - STEP_SIZE * sums


def exchanged(rows, each):
    width = rows.shape[1]
    moved = lax.all_to_all(rows.reshape(-1, each, width), EXPERT, split_axis=0, concat_axis=0, tiled=True)
    return moved.reshape(-1, width)


def swapped(shard):
    return lax.ppermute(shard, "dp", [(0, 1), (1, 0)])


def far(array):
    return pltpu.with_memory_space_constraint(array, pltpu.HBM)


def shapes(*items):
    return tuple(jax.ShapeDtypeStruct(shape, dtype) for shape, dtype in items)


def on_device(
    pooled,
    routes,
    labels,
    in_weight,
    out_weight,
    gate_weight,
    tower_weight,
    tower_bias,
    bag_rows,
    bag_sample,
    bag_weight,
    row_table,
):
    owners = lax.axis_size(EXPERT)
    tok, feature = pooled.shape
    hidden = in_weight.shape[1]
    half = hidden // lax.axis_size("dp")
    rows = ROWS * owners
    slots = 2 * BLOCKS * rows
    in_matrix, out_matrix = in_weight[0], out_weight[0]
    gate_flat = gate_weight.reshape(-1, feature)
    routes_t = routes.T
    in_vmem = pl.BlockSpec(memory_space=pltpu.VMEM)
    in_hbm = pl.BlockSpec(memory_space=pltpu.HBM)
    outbound = call(
        dispatch_kernel,
        jax.ShapeDtypeStruct((rows, BLOCKS * feature), BF),
        (far(routes_t), far(pooled)),
        1 << 27,
        "dispatch",
        4,
        in_specs=[in_hbm, in_hbm],
        out_specs=in_vmem,
        scratch_shapes=[
            pltpu.VMEM(routes_t.shape, jnp.int32),
            pltpu.VMEM(pooled.shape, BF),
            pltpu.SemaphoreType.DMA((2,)),
        ],
    )
    received = exchanged(outbound, ROWS)
    tall = 8 * owners
    take, put, gate_rows, lanes, side, bag_pick, bag_scale = call(
        prepare_kernel,
        shapes(
            ((2 * BLOCKS, tok, rows), BF),
            ((2 * SLOTS, owners, tok), BF),
            ((2, tok, feature), F32),
            ((2, tok, 128), F32),
            ((owners, 128), F32),
            ((tall, tok), BF),
            ((tall, 128), F32),
        ),
        (
            routes,
            routes_t,
            pooled,
            gate_flat,
            labels,
            bag_rows.reshape(owners, ENTRIES),
            bag_sample.reshape(owners, ENTRIES),
            bag_weight.reshape(owners, ENTRIES),
        ),
        1 << 31,
        "prepare",
        60,
    )
    depth = hidden // 2
    slopes = call(
        slope_kernel,
        jax.ShapeDtypeStruct((2, hidden), F32),
        (out_matrix, tower_weight),
        1 << 31,
        "slopes",
        60,
        grid=(hidden // depth,),
        in_specs=[pl.BlockSpec((depth, feature), lambda i: (i, 0)), full(tower_weight.shape)],
        out_specs=pl.BlockSpec((2, depth), lambda i: (0, i)),
    )
    message = call(
        expert_kernel,
        jax.ShapeDtypeStruct((rows, 3 * BLOCKS * feature), BF),
        (received, in_matrix, far(out_matrix), slopes, far(side)),
        7 << 30,
        "expert",
        40,
        in_specs=[in_vmem, in_vmem, in_hbm, in_vmem, pl.BlockSpec(memory_space=pl.ANY)],
        out_specs=in_vmem,
        scratch_shapes=[
            pltpu.VMEM((BLOCKS * rows, 3 * feature), F32),
            pltpu.VMEM((BLOCKS * rows, feature), BF),
            pltpu.VMEM((hidden, feature), BF),
            pltpu.SemaphoreType.DMA((hidden // CHUNK,)),
        ],
    )
    returned = exchanged(message, ROWS)
    received_other = swapped(received)
    tile = 512
    tiles = half // tile
    which = jnp.full((1,), lax.axis_index("dp"), jnp.int32)
    act_t, grad_t, slope = call(
        half_kernel,
        shapes(((half, slots), BF), ((half, slots), BF), ((half, 128), F32)),
        (which, received, received_other, in_matrix, out_matrix, tower_weight),
        7 << 30,
        "half",
        56,
        grid_spec=pltpu.PrefetchScalarGridSpec(
            num_scalar_prefetch=1,
            grid=(tiles,),
            in_specs=[
                full(received.shape),
                full(received.shape),
                pl.BlockSpec((tile, feature), lambda i, part: (part[0] * tiles + i, 0)),
                pl.BlockSpec((tile, feature), lambda i, part: (part[0] * tiles + i, 0)),
                full(tower_weight.shape),
            ],
            out_specs=[
                pl.BlockSpec((tile, slots), lambda i, part: (i, 0)),
                pl.BlockSpec((tile, slots), lambda i, part: (i, 0)),
                pl.BlockSpec((tile, 128), lambda i, part: (i, 0)),
            ],
        ),
    )
    sent = call(
        sample_kernel,
        jax.ShapeDtypeStruct((tall, feature), BF),
        (
            returned,
            take,
            far(put),
            far(gate_rows),
            far(lanes),
            far(side),
            far(bag_pick),
            far(bag_scale),
            tower_weight,
            tower_bias,
            far(slope),
        ),
        1 << 29,
        "sample",
        16,
        in_specs=[in_vmem] * 2 + [in_hbm] * 6 + [in_vmem]
        + [pl.BlockSpec(memory_space=pltpu.SMEM), pl.BlockSpec(memory_space=pl.ANY)],
        out_specs=in_vmem,
        scratch_shapes=[
            pltpu.VMEM(put.shape, BF),
            pltpu.VMEM(gate_rows.shape, F32),
            pltpu.VMEM(lanes.shape, F32),
            pltpu.VMEM(side.shape, F32),
            pltpu.VMEM(bag_pick.shape, BF),
            pltpu.VMEM(bag_scale.shape, F32),
            pltpu.SemaphoreType.DMA((6,)),
        ],
    )
    got = exchanged(sent, 8)
    got_other = swapped(got)
    table_tile = row_table.shape[0] // tiles
    in_grad, out_grad, gate_grad, tower_grad, new_table = call(
        final_kernel,
        shapes(
            ((half, feature), F32),
            ((half, feature), F32),
            ((2, feature), F32),
            ((2, feature), F32),
            (row_table.shape, F32),
        ),
        (received, received_other, got, got_other, far(act_t), far(grad_t), slope, tower_weight, row_table),
        6 << 30,
        "final",
        40,
        grid=(tiles,),
        in_specs=[
            full(received.shape),
            full(received.shape),
            full(got.shape),
            full(got.shape),
            in_hbm,
            in_hbm,
            pl.BlockSpec((tile, 128), lambda i: (i, 0)),
            full(tower_weight.shape),
            pl.BlockSpec((table_tile, feature), lambda i: (i, 0)),
        ],
        out_specs=[
            pl.BlockSpec((tile, feature), lambda i: (i, 0)),
            pl.BlockSpec((tile, feature), lambda i: (i, 0)),
            full((2, feature)),
            full((2, feature)),
            pl.BlockSpec((table_tile, feature), lambda i: (i, 0)),
        ],
        scratch_shapes=[
            pltpu.VMEM((slots, 2 * feature), BF),
            pltpu.VMEM((slots, feature), BF),
            pltpu.VMEM((16, tall), F32),
            pltpu.VMEM((half, slots), BF),
            pltpu.VMEM((half, slots), BF),
            pltpu.SemaphoreType.DMA((2, tiles)),
        ],
    )
    return (in_grad[None], out_grad[None], gate_grad[None], tower_grad, new_table)


def solution(mesh):
    split = Mesh(
        mesh.devices.reshape(4, 8, 4, mesh.shape["dp"]), ("expert_0", "expert_1", "expert_2", "dp")
    )
    in_specs = (
        P(EXPERT_DP, None),
        P(EXPERT_DP, None),
        P(EXPERT_DP, None),
        P(EXPERT, None, None),
        P(EXPERT, None, None),
        P(),
        P(),
        P(),
        P(EXPERT_DP),
        P(EXPERT_DP),
        P(EXPERT_DP),
        P(EXPERT, None),
    )
    out_specs = (
        P(EXPERT, "dp", None),
        P(EXPERT, "dp", None),
        P(EXPERT, None, None),
        P(),
        P(EXPERT, None),
    )
    return jax.shard_map(
        on_device, mesh=split, in_specs=in_specs, out_specs=out_specs, check_vma=False
    )
```

```python
import functools

import jax
import jax.numpy as jnp
from jax import lax
from jax.experimental import pallas as pl
from jax.experimental.pallas import tpu as pltpu
from jax.sharding import Mesh
from jax.sharding import PartitionSpec as P

EXPERT = ("expert_0", "expert_1", "expert_2")
EXPERT_DP = ("expert_0", "expert_1", "expert_2", "dp")

LOSS_SCALE = 32.0
STEP_SIZE = 0.25
BF = jnp.bfloat16
F32 = jnp.float32
CHUNK = 2048

ROWS = 2
BLOCKS = 3
PIECES = 3
SLOT_LANES = 4 * PIECES
SLOTS = ROWS * BLOCKS
ROW_LANES = SLOTS * SLOT_LANES
ENTRIES = 4
SIDE_ROW = 4
TOWER_ROW = 5


def dot(left, right):
    return jnp.dot(left, right, preferred_element_type=F32)


def dot_last(left, right):
    return lax.dot_general(left, right, (((1,), (1,)), ((), ())), preferred_element_type=F32)


def iota(shape, dim):
    return lax.broadcasted_iota(jnp.int32, shape, dim)


def ones_where(mask):
    return jnp.where(mask, 1.0, 0.0).astype(BF)


def three_pieces(value):
    high = value.astype(BF)
    rest = value - high.astype(F32)
    middle = rest.astype(BF)
    low = (rest - middle.astype(F32)).astype(BF)
    return high, middle, low


def tower_pieces(tower):
    pieces = three_pieces(tower)
    row = iota((8, tower.shape[1]), 0)
    stacked = jnp.zeros((8, tower.shape[1]), F32)
    for p, piece in enumerate(pieces):
        for t in range(2):
            stacked = jnp.where(row == 2 * p + t, piece[t : t + 1].astype(F32), stacked)
    return stacked.astype(BF)


def silu_and_slope(pre):
    sigma = 0.5 * jnp.tanh(0.5 * pre) + 0.5
    act = pre * sigma
    return act, sigma + act * (1.0 - sigma)


def full(shape):
    return pl.BlockSpec(shape, lambda *_: (0,) * len(shape))


def call(kernel, out_shape, ins, flops, name, mib, **more):
    return pl.pallas_call(
        kernel,
        out_shape=out_shape,
        cost_estimate=pl.CostEstimate(flops=flops, transcendentals=0, bytes_accessed=1 << 20),
        name=name,
        compiler_params=pltpu.CompilerParams(vmem_limit_bytes=mib << 20),
        **more,
    )(*ins)


def dispatch_kernel(routes_far, pooled_far, out, routes_t, pooled, sems):
    pairs = ((routes_far, routes_t), (pooled_far, pooled))
    copies = [pltpu.make_async_copy(far, near, sems.at[m]) for m, (far, near) in enumerate(pairs)]
    for copy in copies:
        copy.start()
    tok = pooled.shape[0]
    copies[0].wait()
    shape = (out.shape[0], tok)
    row = iota(shape, 0)
    owner = row >> 1
    named = (owner == routes_t[0:1, :]) | (owner == routes_t[1:2, :])
    earlier = ones_where(iota((tok, tok), 0) < iota((tok, tok), 1))
    rank = dot(ones_where(named), earlier)
    first = (BLOCKS * (row & 1)).astype(F32)
    feature = pooled.shape[1]
    copies[1].wait()
    for c in range(BLOCKS):
        pick = ones_where(named & (rank == first + c))
        out[:, c * feature : (c + 1) * feature] = dot(pick, pooled[...]).astype(BF)


def prepare_kernel(
    routes, routes_t, pooled, gate_flat, labels, bag_rows, bag_sample, bag_weight,
    take, put, gate_rows, lanes, side, bag_pick, bag_scale,
):
    tok = pooled.shape[0]
    rows = gate_flat.shape[0]
    owners = bag_rows.shape[0]
    row = iota((tok, rows), 1)
    named = [(row >> 1) == routes[:, k : k + 1] for k in range(2)]
    earlier = ones_where(iota((tok, tok), 0) > iota((tok, tok), 1))
    rank = dot(earlier, ones_where(named[0] | named[1]))
    first = (BLOCKS * (row & 1)).astype(F32)
    for k in range(2):
        for c in range(BLOCKS):
            take[BLOCKS * k + c] = ones_where(named[k] & (rank == first + c))
    owner = iota((owners, tok), 0)
    named_t = [owner == routes_t[k : k + 1, :] for k in range(2)]
    later = ones_where(iota((tok, tok), 0) < iota((tok, tok), 1))
    rank_t = dot(ones_where(named_t[0] | named_t[1]), later)
    for k in range(2):
        for j in range(SLOTS):
            put[SLOTS * k + j] = ones_where(named_t[k] & (rank_t == float(j)))
    logits = dot_last(pooled[...], gate_flat[...])
    lane = iota((tok, 128), 1)
    gate = jnp.zeros((tok, 128), F32)
    label = jnp.zeros((tok, 128), F32)
    for t in range(2):
        of_task = (row & 1) == t
        chosen = [
            jnp.sum(jnp.where(named[k] & of_task, logits, 0.0), axis=1, keepdims=True)
            for k in range(2)
        ]
        gate = jnp.where(lane == t, jax.nn.sigmoid(chosen[0] - chosen[1]), gate)
        label = jnp.where(lane == t, labels[:, t : t + 1].astype(F32), label)
        signs = jnp.where(named[0] & of_task, 1.0, jnp.where(named[1] & of_task, -1.0, 0.0))
        gate_rows[t] = dot(signs.astype(BF), gate_flat[...])
    lanes[0] = gate
    lanes[1] = label
    numbers = jnp.zeros((owners, 128), jnp.int32)
    side_lane = iota((owners, 128), 1)
    for r in range(ENTRIES):
        number = bag_rows[:, r : r + 1]
        numbers = jnp.where(side_lane == ROW_LANES + 2 * r, number >> 8, numbers)
        numbers = jnp.where(side_lane == ROW_LANES + 2 * r + 1, number & 255, numbers)
    side[...] = numbers.astype(F32)
    tall = bag_pick.shape[0]
    spread = ones_where((iota((tall, owners), 0) >> 3) == iota((tall, owners), 1))
    entry = iota((tall, ENTRIES), 0) & 7
    mine = entry == iota((tall, ENTRIES), 1)

    def column(value):
        spread_out = sum(dot(spread, piece) for piece in three_pieces(value))
        return jnp.sum(jnp.where(mine, spread_out, 0.0), axis=1, keepdims=True)

    sample = column(bag_sample[...].astype(F32))
    tall_iota = iota((tall, tok), 0) & 7
    hit = (sample == iota((tall, tok), 1).astype(F32)) & (tall_iota < ENTRIES)
    bag_pick[...] = ones_where(hit)
    bag_scale[...] = jnp.broadcast_to(column(bag_weight[...]), bag_scale.shape)


def slope_kernel(w_out, tower, slopes):
    found = dot_last(tower_pieces(tower[...]), w_out[...])
    for t in range(2):
        slopes[t : t + 1, :] = found[t : t + 1] + found[2 + t : 3 + t] + found[4 + t : 5 + t]


def expert_kernel(x, w_in, w_out_far, slopes, out, total, stacked, w_out, sems):
    rows = x.shape[0]
    hidden, feature = w_out.shape
    wide = 3 * feature
    units = [slice(at, at + CHUNK) for at in range(0, hidden, CHUNK)]
    arrived = []
    for n, unit in enumerate(units):
        copy = pltpu.make_async_copy(w_out_far.at[unit, :], w_out.at[unit, :], sems.at[n])
        copy.start()
        arrived.append(copy)
    for c in range(BLOCKS):
        stacked[c * rows : (c + 1) * rows, :] = x[:, c * feature : (c + 1) * feature]
    for n, unit in enumerate(units):
        act, grad = silu_and_slope(dot_last(stacked[...], w_in[unit, :]))
        parts = [
            dot((grad * slopes[t : t + 1, unit]).astype(BF), w_in[unit, :]) for t in range(2)
        ]
        act = act.astype(BF)
        arrived[n].wait()
        parts = [dot(act, w_out[unit, :])] + parts
        for p, part in enumerate(parts):
            cols = slice(p * feature, (p + 1) * feature)
            if n == 0:
                total[:, cols] = part
            else:
                total[:, cols] += part
    for c in range(BLOCKS):
        out[:, c * wide : (c + 1) * wide] = total[c * rows : (c + 1) * rows, :].astype(BF)


def half_kernel(half, x, x_other, w_in, w_out, tower, act_t, grad_t, slope):
    del half
    feature = w_in.shape[1]
    rows = x.shape[0]
    slopes = dot_last(w_out[...], tower_pieces(tower[...]))
    lane = iota(slope.shape, 1)
    wide = jnp.zeros(slope.shape, F32)
    for t in range(2):
        column = slopes[:, t : t + 1] + slopes[:, 2 + t : 3 + t] + slopes[:, 4 + t : 5 + t]
        wide = jnp.where(lane == t, column, wide)
    slope[...] = wide
    for r, source in enumerate((x, x_other)):
        for c in range(BLOCKS):
            pre = dot_last(w_in[...], source[:, c * feature : (c + 1) * feature])
            act, grad = silu_and_slope(pre)
            at = (BLOCKS * r + c) * rows
            act_t[:, at : at + rows] = act.astype(BF)
            grad_t[:, at : at + rows] = grad.astype(BF)


def sample_kernel(
    back, take_far, put_far, gate_rows_far, lanes_far, side_far, bag_pick_far, bag_scale_far,
    tower, bias, after,
    out, take, put, gate_rows, lanes, side, bag_pick, bag_scale, sems,
):
    del after
    pairs = (
        (take_far, take),
        (lanes_far, lanes),
        (gate_rows_far, gate_rows),
        (bag_pick_far, bag_pick),
        (bag_scale_far, bag_scale),
        (put_far, put),
        (side_far, side),
    )
    copies = [pltpu.make_async_copy(far, near, sems.at[m]) for m, (far, near) in enumerate(pairs)]
    for copy in copies:
        copy.start()
    feature = tower.shape[1]
    wide = 3 * feature
    parts = []
    copies[0].wait()
    for k in range(2):
        part = dot(take[BLOCKS * k], back[:, :wide])
        for c in range(1, BLOCKS):
            part += dot(take[BLOCKS * k + c], back[:, c * wide : (c + 1) * wide])
        parts.append(part)
    task_row = iota((128, feature), 0)
    weights = [
        jnp.where(task_row == 0, piece[0:1].astype(F32), jnp.where(task_row == 1, piece[1:2].astype(F32), 0.0)).astype(BF)
        for piece in three_pieces(tower[...])
    ]
    along = []
    for k in range(2):
        result = parts[k][:, :feature].astype(BF)
        along.append(sum(dot_last(result, weight) for weight in weights))
    for copy in copies[1:]:
        copy.wait()
    first, label = lanes[0], lanes[1]
    second = 1.0 - first
    lane = iota(first.shape, 1)
    lane_bias = jnp.where(lane == 0, bias[0], bias[1])
    logit = first * along[0] + second * along[1] + lane_bias
    logit_grad = jnp.where(lane < 2, LOSS_SCALE * (jax.nn.sigmoid(logit) - label), 0.0)
    pulls = [first * logit_grad, second * logit_grad]
    first_grad = logit_grad * (along[0] - along[1]) * first * second
    pooled_grad = first_grad[:, 0:1] * gate_rows[0] + first_grad[:, 1:2] * gate_rows[1]
    towers = [0.0, 0.0]
    for k in range(2):
        for t in range(2):
            pull = jnp.broadcast_to(pulls[k][:, t : t + 1], (first.shape[0], feature))
            pooled_grad += pull * parts[k][:, (1 + t) * feature : (2 + t) * feature]
            towers[t] += jnp.sum(pull * parts[k][:, :feature], axis=0, keepdims=True)
    picked = sum(dot(bag_pick[...], piece) for piece in three_pieces(pooled_grad))
    placed = [None] * SLOTS
    for k in range(2):
        signed = first_grad if k == 0 else -first_grad
        packed = 0.0
        for kind, value in enumerate((pulls[k], signed)):
            for p, piece in enumerate(three_pieces(value)):
                piece = piece.astype(F32)
                shift = 2 * PIECES * kind + 2 * p
                packed += pltpu.roll(piece, shift, 1) if shift else piece
        packed = packed.astype(BF)
        for j in range(SLOTS):
            part = dot(put[SLOTS * k + j], packed)
            placed[j] = part if k == 0 else placed[j] + part
    extra = side[...] + placed[0]
    for j in range(1, SLOTS):
        extra += pltpu.roll(placed[j], j * SLOT_LANES, 1)
    tall, owners = bag_pick.shape[0], side.shape[0]
    spread = ones_where(iota((tall, owners), 0) == 8 * iota((tall, owners), 1) + SIDE_ROW)
    extra = dot(spread, extra.astype(BF))
    which = iota((tall, 128), 0) & 7
    for at in range(0, feature, 128):
        cols = slice(at, at + 128)
        value = bag_scale[...] * picked[:, cols]
        for t in range(2):
            value = jnp.where(which == TOWER_ROW + t, towers[t][:, cols], value)
        out[:, cols] = (value + extra if at == 0 else value).astype(BF)


def decode(inputs, source, tower, scaled, routed):
    feature = tower.shape[1]
    rows, tall = inputs.shape[0], source.shape[0]
    row = iota((rows, tall), 0)
    expand = ones_where(iota((rows, tall), 1) == 8 * (row >> 1) + SIDE_ROW)
    lane = iota((rows, 128), 1)
    half_lanes = BLOCKS * SLOT_LANES
    odd = (iota((rows, 128), 0) & 1) == 1
    own = (odd & (lane >= half_lanes) & (lane < ROW_LANES)) | (~odd & (lane < half_lanes))
    source_lane = iota((128, feature), 0)
    within = jnp.where(source_lane >= half_lanes, source_lane - half_lanes, source_lane)
    side = jnp.where(own, dot(expand, source[:, :128]), 0.0).astype(BF)
    gate_total = [jnp.zeros((1, feature), F32) for _ in range(2)]
    for c in range(BLOCKS):
        values = []
        for v in range(4):
            base = c * SLOT_LANES + 2 * PIECES * (v // 2) + v % 2
            values.append(dot(side, ones_where((within == base) | (within == base + 2) | (within == base + 4))))
        block = inputs[:, c * feature : (c + 1) * feature].astype(F32)
        at = slice(c * rows, (c + 1) * rows)
        routed[at, :] = (values[0] * tower[0:1, :] + values[1] * tower[1:2, :]).astype(BF)
        for t in range(2):
            scaled[at, t * feature : (t + 1) * feature] = (values[t] * block).astype(BF)
            gate_total[t] += jnp.sum(values[2 + t] * block, axis=0, keepdims=True)
    tower_pick = ones_where((iota((8, tall), 1) & 7) == TOWER_ROW + iota((8, tall), 0))
    tower_total = dot(tower_pick, source[...])
    wanted, asked = iota((8, 128), 1), iota((8, 128), 0)
    select = jnp.where(wanted == ROW_LANES + 2 * asked, 256.0, 0.0)
    select = jnp.where(wanted == ROW_LANES + 2 * asked + 1, 1.0, select).astype(BF)
    numbers = dot_last(select, source[:, :128])
    which = iota((1, tall), 1) & 7
    target = jnp.full((1, tall), -1.0, F32)
    for e in range(ENTRIES):
        moved = pltpu.roll(numbers, tall + e - SIDE_ROW, 1)
        target = jnp.where(which == e, moved[e : e + 1], target)
    return gate_total, tower_total, target


def row_sums(target, source, start, depth):
    number = (start + iota((depth, source.shape[0]), 0)).astype(F32)
    return dot(ones_where(number == target), source[...])


def own_kernel(x, got, tower, table, scaled, routed, gate_part, tower_part, table_part):
    gate_total, tower_total, target = decode(x, got, tower, scaled, routed)
    for t in range(2):
        gate_part[t : t + 1, :] = gate_total[t]
        tower_part[t : t + 1, :] = tower_total[t : t + 1]
    depth = 256
    for start in range(0, table.shape[0], depth):
        at = slice(start, start + depth)
        table_part[at, :] = table[at, :] - STEP_SIZE * row_sums(target, got, start, depth)


def final_kernel(
    x_other, got_other, scaled_own, routed_own, act_far, grad_far, slope, tower,
    gate_part, tower_part, table_part,
    in_grad, out_grad, gate_grad, tower_grad, new_table,
    scaled, routed, targets, act_t, grad_t, sems,
):
    feature = tower.shape[1]
    step = pl.program_id(0)
    tile = in_grad.shape[0]

    def arriving(n):
        part = pl.ds(n * tile, tile)
        pairs = ((grad_far, grad_t), (act_far, act_t))
        return [
            pltpu.make_async_copy(distant.at[part, :], near.at[part, :], sems.at[m, n])
            for m, (distant, near) in enumerate(pairs)
        ]

    @pl.when(step == 0)
    def _():
        for n in range(act_t.shape[0] // tile):
            for copy in arriving(n):
                copy.start()
        gate_total, tower_total, target = decode(x_other, got_other, tower, scaled, routed)
        targets[...] = jnp.broadcast_to(target, targets.shape)
        for t in range(2):
            gate_grad[t : t + 1, :] = gate_part[t : t + 1, :] + gate_total[t]
            tower_grad[t : t + 1, :] = tower_part[t : t + 1, :] + tower_total[t : t + 1]

    for copy in arriving(step):
        copy.wait()
    part = pl.ds(pl.multiple_of(step * tile, tile), tile)
    split = scaled.shape[0]
    both = dot(grad_t[part, :split], scaled_own[...]) + dot(grad_t[part, split:], scaled[...])
    in_grad[...] = slope[:, 0:1] * both[:, :feature] + slope[:, 1:2] * both[:, feature:]
    out_grad[...] = dot(act_t[part, :split], routed_own[...]) + dot(act_t[part, split:], routed[...])
    depth = new_table.shape[0]
    sums = row_sums(targets[0:1, :], got_other, step * depth, depth)
    new_table[...] = table_part[...] - STEP_SIZE * sums


def exchanged(rows, each):
    width = rows.shape[1]
    moved = lax.all_to_all(rows.reshape(-1, each, width), EXPERT, split_axis=0, concat_axis=0, tiled=True)
    return moved.reshape(-1, width)


def swapped(shard):
    return lax.ppermute(shard, "dp", [(0, 1), (1, 0)])


def far(array):
    return pltpu.with_memory_space_constraint(array, pltpu.HBM)


def shapes(*items):
    return tuple(jax.ShapeDtypeStruct(shape, dtype) for shape, dtype in items)


def on_device(
    pooled,
    routes,
    labels,
    in_weight,
    out_weight,
    gate_weight,
    tower_weight,
    tower_bias,
    bag_rows,
    bag_sample,
    bag_weight,
    row_table,
):
    owners = lax.axis_size(EXPERT)
    tok, feature = pooled.shape
    hidden = in_weight.shape[1]
    half = hidden // lax.axis_size("dp")
    rows = ROWS * owners
    slots = 2 * BLOCKS * rows
    in_matrix, out_matrix = in_weight[0], out_weight[0]
    gate_flat = gate_weight.reshape(-1, feature)
    routes_t = routes.T
    in_vmem = pl.BlockSpec(memory_space=pltpu.VMEM)
    in_hbm = pl.BlockSpec(memory_space=pltpu.HBM)
    outbound = call(
        dispatch_kernel,
        jax.ShapeDtypeStruct((rows, BLOCKS * feature), BF),
        (far(routes_t), far(pooled)),
        1 << 27,
        "dispatch",
        4,
        in_specs=[in_hbm, in_hbm],
        out_specs=in_vmem,
        scratch_shapes=[
            pltpu.VMEM(routes_t.shape, jnp.int32),
            pltpu.VMEM(pooled.shape, BF),
            pltpu.SemaphoreType.DMA((2,)),
        ],
    )
    received = exchanged(outbound, ROWS)
    tall = 8 * owners
    take, put, gate_rows, lanes, side, bag_pick, bag_scale = call(
        prepare_kernel,
        shapes(
            ((2 * BLOCKS, tok, rows), BF),
            ((2 * SLOTS, owners, tok), BF),
            ((2, tok, feature), F32),
            ((2, tok, 128), F32),
            ((owners, 128), F32),
            ((tall, tok), BF),
            ((tall, 128), F32),
        ),
        (
            routes,
            routes_t,
            pooled,
            gate_flat,
            labels,
            bag_rows.reshape(owners, ENTRIES),
            bag_sample.reshape(owners, ENTRIES),
            bag_weight.reshape(owners, ENTRIES),
        ),
        1 << 31,
        "prepare",
        60,
    )
    depth = hidden // 2
    slopes = call(
        slope_kernel,
        jax.ShapeDtypeStruct((2, hidden), F32),
        (out_matrix, tower_weight),
        1 << 31,
        "slopes",
        60,
        grid=(hidden // depth,),
        in_specs=[pl.BlockSpec((depth, feature), lambda i: (i, 0)), full(tower_weight.shape)],
        out_specs=pl.BlockSpec((2, depth), lambda i: (0, i)),
    )
    message = call(
        expert_kernel,
        jax.ShapeDtypeStruct((rows, 3 * BLOCKS * feature), BF),
        (received, in_matrix, far(out_matrix), slopes),
        7 << 30,
        "expert",
        40,
        in_specs=[in_vmem, in_vmem, in_hbm, in_vmem],
        out_specs=in_vmem,
        scratch_shapes=[
            pltpu.VMEM((BLOCKS * rows, 3 * feature), F32),
            pltpu.VMEM((BLOCKS * rows, feature), BF),
            pltpu.VMEM((hidden, feature), BF),
            pltpu.SemaphoreType.DMA((hidden // CHUNK,)),
        ],
    )
    returned = exchanged(message, ROWS)
    received_other = swapped(received)
    tile = 512
    tiles = half // tile
    which = jnp.full((1,), lax.axis_index("dp"), jnp.int32)
    act_t, grad_t, slope = call(
        half_kernel,
        shapes(((half, slots), BF), ((half, slots), BF), ((half, 128), F32)),
        (which, received, received_other, in_matrix, out_matrix, tower_weight),
        7 << 30,
        "half",
        56,
        grid_spec=pltpu.PrefetchScalarGridSpec(
            num_scalar_prefetch=1,
            grid=(tiles,),
            in_specs=[
                full(received.shape),
                full(received.shape),
                pl.BlockSpec((tile, feature), lambda i, part: (part[0] * tiles + i, 0)),
                pl.BlockSpec((tile, feature), lambda i, part: (part[0] * tiles + i, 0)),
                full(tower_weight.shape),
            ],
            out_specs=[
                pl.BlockSpec((tile, slots), lambda i, part: (i, 0)),
                pl.BlockSpec((tile, slots), lambda i, part: (i, 0)),
                pl.BlockSpec((tile, 128), lambda i, part: (i, 0)),
            ],
        ),
    )
    sent = call(
        sample_kernel,
        jax.ShapeDtypeStruct((tall, feature), BF),
        (
            returned,
            far(take),
            far(put),
            far(gate_rows),
            far(lanes),
            far(side),
            far(bag_pick),
            far(bag_scale),
            tower_weight,
            tower_bias,
            far(slope),
        ),
        1 << 29,
        "sample",
        16,
        in_specs=[in_vmem] + [in_hbm] * 7 + [in_vmem]
        + [pl.BlockSpec(memory_space=pltpu.SMEM), pl.BlockSpec(memory_space=pl.ANY)],
        out_specs=in_vmem,
        scratch_shapes=[
            pltpu.VMEM(take.shape, BF),
            pltpu.VMEM(put.shape, BF),
            pltpu.VMEM(gate_rows.shape, F32),
            pltpu.VMEM(lanes.shape, F32),
            pltpu.VMEM(side.shape, F32),
            pltpu.VMEM(bag_pick.shape, BF),
            pltpu.VMEM(bag_scale.shape, F32),
            pltpu.SemaphoreType.DMA((7,)),
        ],
    )
    got = exchanged(sent, 8)
    got_other = swapped(got)
    own_slots = slots // 2
    scaled, routed, gate_part, tower_part, table_part = call(
        own_kernel,
        shapes(
            ((own_slots, 2 * feature), BF),
            ((own_slots, feature), BF),
            ((2, feature), F32),
            ((2, feature), F32),
            (row_table.shape, F32),
        ),
        (received, got, tower_weight, row_table),
        1 << 29,
        "own",
        12,
    )
    table_tile = row_table.shape[0] // tiles
    in_grad, out_grad, gate_grad, tower_grad, new_table = call(
        final_kernel,
        shapes(
            ((half, feature), F32),
            ((half, feature), F32),
            ((2, feature), F32),
            ((2, feature), F32),
            (row_table.shape, F32),
        ),
        (
            received_other,
            got_other,
            scaled,
            routed,
            far(act_t),
            far(grad_t),
            slope,
            tower_weight,
            gate_part,
            tower_part,
            table_part,
        ),
        6 << 30,
        "final",
        40,
        grid=(tiles,),
        in_specs=[
            full(received.shape),
            full(got.shape),
            full(scaled.shape),
            full(routed.shape),
            in_hbm,
            in_hbm,
            pl.BlockSpec((tile, 128), lambda i: (i, 0)),
            full(tower_weight.shape),
            full((2, feature)),
            full((2, feature)),
            pl.BlockSpec((table_tile, feature), lambda i: (i, 0)),
        ],
        out_specs=[
            pl.BlockSpec((tile, feature), lambda i: (i, 0)),
            pl.BlockSpec((tile, feature), lambda i: (i, 0)),
            full((2, feature)),
            full((2, feature)),
            pl.BlockSpec((table_tile, feature), lambda i: (i, 0)),
        ],
        scratch_shapes=[
            pltpu.VMEM((own_slots, 2 * feature), BF),
            pltpu.VMEM((own_slots, feature), BF),
            pltpu.VMEM((8, tall), F32),
            pltpu.VMEM((half, slots), BF),
            pltpu.VMEM((half, slots), BF),
            pltpu.SemaphoreType.DMA((2, tiles)),
        ],
    )
    return (in_grad[None], out_grad[None], gate_grad[None], tower_grad, new_table)


def solution(mesh):
    split = Mesh(
        mesh.devices.reshape(4, 8, 4, mesh.shape["dp"]), ("expert_0", "expert_1", "expert_2", "dp")
    )
    in_specs = (
        P(EXPERT_DP, None),
        P(EXPERT_DP, None),
        P(EXPERT_DP, None),
        P(EXPERT, None, None),
        P(EXPERT, None, None),
        P(),
        P(),
        P(),
        P(EXPERT_DP),
        P(EXPERT_DP),
        P(EXPERT_DP),
        P(EXPERT, None),
    )
    out_specs = (
        P(EXPERT, "dp", None),
        P(EXPERT, "dp", None),
        P(EXPERT, None, None),
        P(),
        P(EXPERT, None),
    )
    return jax.shard_map(
        on_device, mesh=split, in_specs=in_specs, out_specs=out_specs, check_vma=False
    )
```

```python
import functools

import jax
import jax.numpy as jnp
from jax import lax
from jax.experimental import pallas as pl
from jax.experimental.pallas import tpu as pltpu
from jax.sharding import Mesh
from jax.sharding import PartitionSpec as P

EXPERT = ("expert_0", "expert_1", "expert_2")
EXPERT_DP = ("expert_0", "expert_1", "expert_2", "dp")

LOSS_SCALE = 32.0
STEP_SIZE = 0.25
BF = jnp.bfloat16
F32 = jnp.float32

ROWS = 2
BLOCKS = 3
PIECES = 3
SLOT_LANES = 4 * PIECES
SLOTS = ROWS * BLOCKS
ROW_LANES = SLOTS * SLOT_LANES
ENTRIES = 4
SIDE_ROW = 4
TOWER_ROW = 5


def dot(left, right):
    return jnp.dot(left, right, preferred_element_type=F32)


def dot_last(left, right):
    return lax.dot_general(left, right, (((1,), (1,)), ((), ())), preferred_element_type=F32)


def iota(shape, dim):
    return lax.broadcasted_iota(jnp.int32, shape, dim)


def ones_where(mask):
    return jnp.where(mask, 1.0, 0.0).astype(BF)


def three_pieces(value):
    high = value.astype(BF)
    rest = value - high.astype(F32)
    middle = rest.astype(BF)
    low = (rest - middle.astype(F32)).astype(BF)
    return high, middle, low


def tower_pieces(tower):
    pieces = three_pieces(tower)
    row = iota((8, tower.shape[1]), 0)
    stacked = jnp.zeros((8, tower.shape[1]), F32)
    for p, piece in enumerate(pieces):
        for t in range(2):
            stacked = jnp.where(row == 2 * p + t, piece[t : t + 1].astype(F32), stacked)
    return stacked.astype(BF)


def silu_and_slope(pre):
    sigma = 0.5 * jnp.tanh(0.5 * pre) + 0.5
    act = pre * sigma
    return act, sigma + act * (1.0 - sigma)


def full(shape):
    return pl.BlockSpec(shape, lambda *_: (0,) * len(shape))


def call(kernel, out_shape, ins, flops, name, mib, **more):
    return pl.pallas_call(
        kernel,
        out_shape=out_shape,
        cost_estimate=pl.CostEstimate(flops=flops, transcendentals=0, bytes_accessed=1 << 20),
        name=name,
        compiler_params=pltpu.CompilerParams(vmem_limit_bytes=mib << 20),
        **more,
    )(*ins)


def dispatch_kernel(routes_far, pooled_far, out, routes_t, pooled, sems):
    pairs = ((routes_far, routes_t), (pooled_far, pooled))
    copies = [pltpu.make_async_copy(far, near, sems.at[m]) for m, (far, near) in enumerate(pairs)]
    for copy in copies:
        copy.start()
    tok = pooled.shape[0]
    copies[0].wait()
    shape = (out.shape[0], tok)
    row = iota(shape, 0)
    owner = row >> 1
    named = (owner == routes_t[0:1, :]) | (owner == routes_t[1:2, :])
    earlier = ones_where(iota((tok, tok), 0) < iota((tok, tok), 1))
    rank = dot(ones_where(named), earlier)
    first = (BLOCKS * (row & 1)).astype(F32)
    feature = pooled.shape[1]
    copies[1].wait()
    for c in range(BLOCKS):
        pick = ones_where(named & (rank == first + c))
        out[:, c * feature : (c + 1) * feature] = dot(pick, pooled[...]).astype(BF)


def prepare_kernel(
    routes, routes_t, pooled, gate_flat, labels, bag_rows, bag_sample, bag_weight,
    take, put, gate_rows, lanes, side, bag_pick, bag_scale,
):
    tok = pooled.shape[0]
    rows = gate_flat.shape[0]
    owners = bag_rows.shape[0]
    row = iota((tok, rows), 1)
    named = [(row >> 1) == routes[:, k : k + 1] for k in range(2)]
    earlier = ones_where(iota((tok, tok), 0) > iota((tok, tok), 1))
    rank = dot(earlier, ones_where(named[0] | named[1]))
    first = (BLOCKS * (row & 1)).astype(F32)
    for k in range(2):
        for c in range(BLOCKS):
            take[BLOCKS * k + c] = ones_where(named[k] & (rank == first + c))
    owner = iota((owners, tok), 0)
    named_t = [owner == routes_t[k : k + 1, :] for k in range(2)]
    later = ones_where(iota((tok, tok), 0) < iota((tok, tok), 1))
    rank_t = dot(ones_where(named_t[0] | named_t[1]), later)
    for k in range(2):
        for j in range(SLOTS):
            put[SLOTS * k + j] = ones_where(named_t[k] & (rank_t == float(j)))
    logits = dot_last(pooled[...], gate_flat[...])
    lane = iota((tok, 128), 1)
    gate = jnp.zeros((tok, 128), F32)
    label = jnp.zeros((tok, 128), F32)
    for t in range(2):
        of_task = (row & 1) == t
        chosen = [
            jnp.sum(jnp.where(named[k] & of_task, logits, 0.0), axis=1, keepdims=True)
            for k in range(2)
        ]
        gate = jnp.where(lane == t, jax.nn.sigmoid(chosen[0] - chosen[1]), gate)
        label = jnp.where(lane == t, labels[:, t : t + 1].astype(F32), label)
        signs = jnp.where(named[0] & of_task, 1.0, jnp.where(named[1] & of_task, -1.0, 0.0))
        gate_rows[t] = dot(signs.astype(BF), gate_flat[...])
    lanes[0] = gate
    lanes[1] = label
    numbers = jnp.zeros((owners, 128), jnp.int32)
    side_lane = iota((owners, 128), 1)
    for r in range(ENTRIES):
        number = bag_rows[:, r : r + 1]
        numbers = jnp.where(side_lane == ROW_LANES + 2 * r, number >> 8, numbers)
        numbers = jnp.where(side_lane == ROW_LANES + 2 * r + 1, number & 255, numbers)
    side[...] = numbers.astype(F32)
    tall = bag_pick.shape[0]
    spread = ones_where((iota((tall, owners), 0) >> 3) == iota((tall, owners), 1))
    entry = iota((tall, ENTRIES), 0) & 7
    mine = entry == iota((tall, ENTRIES), 1)

    def column(value):
        spread_out = sum(dot(spread, piece) for piece in three_pieces(value))
        return jnp.sum(jnp.where(mine, spread_out, 0.0), axis=1, keepdims=True)

    sample = column(bag_sample[...].astype(F32))
    tall_iota = iota((tall, tok), 0) & 7
    hit = (sample == iota((tall, tok), 1).astype(F32)) & (tall_iota < ENTRIES)
    bag_pick[...] = ones_where(hit)
    bag_scale[...] = jnp.broadcast_to(column(bag_weight[...]), bag_scale.shape)


def slope_kernel(w_out, tower, slopes):
    found = dot_last(tower_pieces(tower[...]), w_out[...])
    for t in range(2):
        slopes[t : t + 1, :] = found[t : t + 1] + found[2 + t : 3 + t] + found[4 + t : 5 + t]


def expert_kernel(x, w_in, w_out, slopes, out, total, stacked):
    step = pl.program_id(0)
    rows = x.shape[0]
    feature = w_in.shape[1]
    wide = 3 * feature

    @pl.when(step == 0)
    def _():
        total[...] = jnp.zeros_like(total)
        for c in range(BLOCKS):
            stacked[c * rows : (c + 1) * rows, :] = x[:, c * feature : (c + 1) * feature]

    act, grad = silu_and_slope(dot_last(stacked[...], w_in[...]))
    total[:, :feature] += dot(act.astype(BF), w_out[...])
    for t in range(2):
        cols = slice((1 + t) * feature, (2 + t) * feature)
        total[:, cols] += dot((grad * slopes[t : t + 1, :]).astype(BF), w_in[...])

    @pl.when(step == pl.num_programs(0) - 1)
    def _():
        for c in range(BLOCKS):
            out[:, c * wide : (c + 1) * wide] = total[c * rows : (c + 1) * rows, :].astype(BF)


def half_kernel(half, x, x_other, w_in, w_out, tower, act_t, grad_t, slope):
    del half
    feature = w_in.shape[1]
    rows = x.shape[0]
    slopes = dot_last(w_out[...], tower_pieces(tower[...]))
    lane = iota(slope.shape, 1)
    wide = jnp.zeros(slope.shape, F32)
    for t in range(2):
        column = slopes[:, t : t + 1] + slopes[:, 2 + t : 3 + t] + slopes[:, 4 + t : 5 + t]
        wide = jnp.where(lane == t, column, wide)
    slope[...] = wide
    for r, source in enumerate((x, x_other)):
        for c in range(BLOCKS):
            pre = dot_last(w_in[...], source[:, c * feature : (c + 1) * feature])
            act, grad = silu_and_slope(pre)
            at = (BLOCKS * r + c) * rows
            act_t[:, at : at + rows] = act.astype(BF)
            grad_t[:, at : at + rows] = grad.astype(BF)


def sample_kernel(
    back, take_far, put_far, gate_rows_far, lanes_far, side_far, bag_pick_far, bag_scale_far,
    tower, bias, after,
    out, take, put, gate_rows, lanes, side, bag_pick, bag_scale, sems,
):
    del after
    pairs = (
        (take_far, take),
        (lanes_far, lanes),
        (gate_rows_far, gate_rows),
        (bag_pick_far, bag_pick),
        (bag_scale_far, bag_scale),
        (put_far, put),
        (side_far, side),
    )
    copies = [pltpu.make_async_copy(far, near, sems.at[m]) for m, (far, near) in enumerate(pairs)]
    for copy in copies:
        copy.start()
    feature = tower.shape[1]
    wide = 3 * feature
    parts = []
    copies[0].wait()
    for k in range(2):
        part = dot(take[BLOCKS * k], back[:, :wide])
        for c in range(1, BLOCKS):
            part += dot(take[BLOCKS * k + c], back[:, c * wide : (c + 1) * wide])
        parts.append(part)
    task_row = iota((128, feature), 0)
    weights = [
        jnp.where(task_row == 0, piece[0:1].astype(F32), jnp.where(task_row == 1, piece[1:2].astype(F32), 0.0)).astype(BF)
        for piece in three_pieces(tower[...])
    ]
    along = []
    for k in range(2):
        result = parts[k][:, :feature].astype(BF)
        along.append(sum(dot_last(result, weight) for weight in weights))
    for copy in copies[1:]:
        copy.wait()
    first, label = lanes[0], lanes[1]
    second = 1.0 - first
    lane = iota(first.shape, 1)
    lane_bias = jnp.where(lane == 0, bias[0], bias[1])
    logit = first * along[0] + second * along[1] + lane_bias
    logit_grad = jnp.where(lane < 2, LOSS_SCALE * (jax.nn.sigmoid(logit) - label), 0.0)
    pulls = [first * logit_grad, second * logit_grad]
    first_grad = logit_grad * (along[0] - along[1]) * first * second
    pooled_grad = first_grad[:, 0:1] * gate_rows[0] + first_grad[:, 1:2] * gate_rows[1]
    towers = [0.0, 0.0]
    for k in range(2):
        for t in range(2):
            pull = jnp.broadcast_to(pulls[k][:, t : t + 1], (first.shape[0], feature))
            pooled_grad += pull * parts[k][:, (1 + t) * feature : (2 + t) * feature]
            towers[t] += jnp.sum(pull * parts[k][:, :feature], axis=0, keepdims=True)
    picked = sum(dot(bag_pick[...], piece) for piece in three_pieces(pooled_grad))
    placed = [None] * SLOTS
    for k in range(2):
        signed = first_grad if k == 0 else -first_grad
        packed = 0.0
        for kind, value in enumerate((pulls[k], signed)):
            for p, piece in enumerate(three_pieces(value)):
                piece = piece.astype(F32)
                shift = 2 * PIECES * kind + 2 * p
                packed += pltpu.roll(piece, shift, 1) if shift else piece
        packed = packed.astype(BF)
        for j in range(SLOTS):
            part = dot(put[SLOTS * k + j], packed)
            placed[j] = part if k == 0 else placed[j] + part
    extra = side[...] + placed[0]
    for j in range(1, SLOTS):
        extra += pltpu.roll(placed[j], j * SLOT_LANES, 1)
    tall, owners = bag_pick.shape[0], side.shape[0]
    spread = ones_where(iota((tall, owners), 0) == 8 * iota((tall, owners), 1) + SIDE_ROW)
    extra = dot(spread, extra.astype(BF))
    which = iota((tall, 128), 0) & 7
    for at in range(0, feature, 128):
        cols = slice(at, at + 128)
        value = bag_scale[...] * picked[:, cols]
        for t in range(2):
            value = jnp.where(which == TOWER_ROW + t, towers[t][:, cols], value)
        out[:, cols] = (value + extra if at == 0 else value).astype(BF)


def decode(inputs, source, tower, scaled, routed):
    feature = tower.shape[1]
    rows, tall = inputs.shape[0], source.shape[0]
    row = iota((rows, tall), 0)
    expand = ones_where(iota((rows, tall), 1) == 8 * (row >> 1) + SIDE_ROW)
    lane = iota((rows, 128), 1)
    half_lanes = BLOCKS * SLOT_LANES
    odd = (iota((rows, 128), 0) & 1) == 1
    own = (odd & (lane >= half_lanes) & (lane < ROW_LANES)) | (~odd & (lane < half_lanes))
    source_lane = iota((128, feature), 0)
    within = jnp.where(source_lane >= half_lanes, source_lane - half_lanes, source_lane)
    side = jnp.where(own, dot(expand, source[:, :128]), 0.0).astype(BF)
    gate_total = [jnp.zeros((1, feature), F32) for _ in range(2)]
    for c in range(BLOCKS):
        values = []
        for v in range(4):
            base = c * SLOT_LANES + 2 * PIECES * (v // 2) + v % 2
            values.append(dot(side, ones_where((within == base) | (within == base + 2) | (within == base + 4))))
        block = inputs[:, c * feature : (c + 1) * feature].astype(F32)
        at = slice(c * rows, (c + 1) * rows)
        routed[at, :] = (values[0] * tower[0:1, :] + values[1] * tower[1:2, :]).astype(BF)
        for t in range(2):
            scaled[at, t * feature : (t + 1) * feature] = (values[t] * block).astype(BF)
            gate_total[t] += jnp.sum(values[2 + t] * block, axis=0, keepdims=True)
    tower_pick = ones_where((iota((8, tall), 1) & 7) == TOWER_ROW + iota((8, tall), 0))
    tower_total = dot(tower_pick, source[...])
    wanted, asked = iota((8, 128), 1), iota((8, 128), 0)
    select = jnp.where(wanted == ROW_LANES + 2 * asked, 256.0, 0.0)
    select = jnp.where(wanted == ROW_LANES + 2 * asked + 1, 1.0, select).astype(BF)
    numbers = dot_last(select, source[:, :128])
    which = iota((1, tall), 1) & 7
    target = jnp.full((1, tall), -1.0, F32)
    for e in range(ENTRIES):
        moved = pltpu.roll(numbers, tall + e - SIDE_ROW, 1)
        target = jnp.where(which == e, moved[e : e + 1], target)
    return gate_total, tower_total, target


def row_sums(target, source, start, depth):
    number = (start + iota((depth, source.shape[0]), 0)).astype(F32)
    return dot(ones_where(number == target), source[...])


def own_kernel(x, got, tower, table, scaled, routed, gate_part, tower_part, table_part):
    gate_total, tower_total, target = decode(x, got, tower, scaled, routed)
    for t in range(2):
        gate_part[t : t + 1, :] = gate_total[t]
        tower_part[t : t + 1, :] = tower_total[t : t + 1]
    depth = 256
    for start in range(0, table.shape[0], depth):
        at = slice(start, start + depth)
        table_part[at, :] = table[at, :] - STEP_SIZE * row_sums(target, got, start, depth)


def final_kernel(
    x_other, got_other, scaled_own, routed_own, act_far, grad_far, slope, tower,
    gate_part, tower_part, table_part,
    in_grad, out_grad, gate_grad, tower_grad, new_table,
    scaled, routed, targets, act_t, grad_t, sems,
):
    feature = tower.shape[1]
    step = pl.program_id(0)
    tile = in_grad.shape[0]

    def arriving(n):
        part = pl.ds(n * tile, tile)
        pairs = ((grad_far, grad_t), (act_far, act_t))
        return [
            pltpu.make_async_copy(distant.at[part, :], near.at[part, :], sems.at[m, n])
            for m, (distant, near) in enumerate(pairs)
        ]

    @pl.when(step == 0)
    def _():
        for n in range(act_t.shape[0] // tile):
            for copy in arriving(n):
                copy.start()
        gate_total, tower_total, target = decode(x_other, got_other, tower, scaled, routed)
        targets[...] = jnp.broadcast_to(target, targets.shape)
        for t in range(2):
            gate_grad[t : t + 1, :] = gate_part[t : t + 1, :] + gate_total[t]
            tower_grad[t : t + 1, :] = tower_part[t : t + 1, :] + tower_total[t : t + 1]

    for copy in arriving(step):
        copy.wait()
    part = pl.ds(pl.multiple_of(step * tile, tile), tile)
    split = scaled.shape[0]
    both = dot(grad_t[part, :split], scaled_own[...]) + dot(grad_t[part, split:], scaled[...])
    in_grad[...] = slope[:, 0:1] * both[:, :feature] + slope[:, 1:2] * both[:, feature:]
    out_grad[...] = dot(act_t[part, :split], routed_own[...]) + dot(act_t[part, split:], routed[...])
    depth = new_table.shape[0]
    sums = row_sums(targets[0:1, :], got_other, step * depth, depth)
    new_table[...] = table_part[...] - STEP_SIZE * sums


def exchanged(rows, each):
    width = rows.shape[1]
    moved = lax.all_to_all(rows.reshape(-1, each, width), EXPERT, split_axis=0, concat_axis=0, tiled=True)
    return moved.reshape(-1, width)


def swapped(shard):
    return lax.ppermute(shard, "dp", [(0, 1), (1, 0)])


def far(array):
    return pltpu.with_memory_space_constraint(array, pltpu.HBM)


def shapes(*items):
    return tuple(jax.ShapeDtypeStruct(shape, dtype) for shape, dtype in items)


def on_device(
    pooled,
    routes,
    labels,
    in_weight,
    out_weight,
    gate_weight,
    tower_weight,
    tower_bias,
    bag_rows,
    bag_sample,
    bag_weight,
    row_table,
):
    owners = lax.axis_size(EXPERT)
    tok, feature = pooled.shape
    hidden = in_weight.shape[1]
    half = hidden // lax.axis_size("dp")
    rows = ROWS * owners
    slots = 2 * BLOCKS * rows
    in_matrix, out_matrix = in_weight[0], out_weight[0]
    gate_flat = gate_weight.reshape(-1, feature)
    routes_t = routes.T
    in_vmem = pl.BlockSpec(memory_space=pltpu.VMEM)
    in_hbm = pl.BlockSpec(memory_space=pltpu.HBM)
    outbound = call(
        dispatch_kernel,
        jax.ShapeDtypeStruct((rows, BLOCKS * feature), BF),
        (far(routes_t), far(pooled)),
        1 << 27,
        "dispatch",
        4,
        in_specs=[in_hbm, in_hbm],
        out_specs=in_vmem,
        scratch_shapes=[
            pltpu.VMEM(routes_t.shape, jnp.int32),
            pltpu.VMEM(pooled.shape, BF),
            pltpu.SemaphoreType.DMA((2,)),
        ],
    )
    received = exchanged(outbound, ROWS)
    tall = 8 * owners
    take, put, gate_rows, lanes, side, bag_pick, bag_scale = call(
        prepare_kernel,
        shapes(
            ((2 * BLOCKS, tok, rows), BF),
            ((2 * SLOTS, owners, tok), BF),
            ((2, tok, feature), F32),
            ((2, tok, 128), F32),
            ((owners, 128), F32),
            ((tall, tok), BF),
            ((tall, 128), F32),
        ),
        (
            routes,
            routes_t,
            pooled,
            gate_flat,
            labels,
            bag_rows.reshape(owners, ENTRIES),
            bag_sample.reshape(owners, ENTRIES),
            bag_weight.reshape(owners, ENTRIES),
        ),
        1 << 31,
        "prepare",
        60,
    )
    depth = hidden // 2
    slopes = call(
        slope_kernel,
        jax.ShapeDtypeStruct((2, hidden), F32),
        (out_matrix, tower_weight),
        1 << 31,
        "slopes",
        12,
        grid=(hidden // depth,),
        in_specs=[pl.BlockSpec((depth, feature), lambda i: (i, 0)), full(tower_weight.shape)],
        out_specs=pl.BlockSpec((2, depth), lambda i: (0, i)),
    )
    piece = hidden // 2
    message = call(
        expert_kernel,
        jax.ShapeDtypeStruct((rows, 3 * BLOCKS * feature), BF),
        (received, far(in_matrix), far(out_matrix), slopes),
        7 << 30,
        "expert",
        32,
        grid=(hidden // piece,),
        in_specs=[
            full(received.shape),
            pl.BlockSpec((piece, feature), lambda i: (i, 0)),
            pl.BlockSpec((piece, feature), lambda i: (i, 0)),
            pl.BlockSpec((2, piece), lambda i: (0, i)),
        ],
        out_specs=full((rows, 3 * BLOCKS * feature)),
        scratch_shapes=[
            pltpu.VMEM((BLOCKS * rows, 3 * feature), F32),
            pltpu.VMEM((BLOCKS * rows, feature), BF),
        ],
    )
    returned = exchanged(message, ROWS)
    received_other = swapped(received)
    tile = 512
    tiles = half // tile
    which = jnp.full((1,), lax.axis_index("dp"), jnp.int32)
    act_t, grad_t, slope = call(
        half_kernel,
        shapes(((half, slots), BF), ((half, slots), BF), ((half, 128), F32)),
        (which, received, received_other, in_matrix, out_matrix, tower_weight),
        7 << 30,
        "half",
        56,
        grid_spec=pltpu.PrefetchScalarGridSpec(
            num_scalar_prefetch=1,
            grid=(tiles,),
            in_specs=[
                full(received.shape),
                full(received.shape),
                pl.BlockSpec((tile, feature), lambda i, part: (part[0] * tiles + i, 0)),
                pl.BlockSpec((tile, feature), lambda i, part: (part[0] * tiles + i, 0)),
                full(tower_weight.shape),
            ],
            out_specs=[
                pl.BlockSpec((tile, slots), lambda i, part: (i, 0)),
                pl.BlockSpec((tile, slots), lambda i, part: (i, 0)),
                pl.BlockSpec((tile, 128), lambda i, part: (i, 0)),
            ],
        ),
    )
    sent = call(
        sample_kernel,
        jax.ShapeDtypeStruct((tall, feature), BF),
        (
            returned,
            far(take),
            far(put),
            far(gate_rows),
            far(lanes),
            far(side),
            far(bag_pick),
            far(bag_scale),
            tower_weight,
            tower_bias,
            far(slope),
        ),
        1 << 29,
        "sample",
        16,
        in_specs=[in_vmem] + [in_hbm] * 7 + [in_vmem]
        + [pl.BlockSpec(memory_space=pltpu.SMEM), pl.BlockSpec(memory_space=pl.ANY)],
        out_specs=in_vmem,
        scratch_shapes=[
            pltpu.VMEM(take.shape, BF),
            pltpu.VMEM(put.shape, BF),
            pltpu.VMEM(gate_rows.shape, F32),
            pltpu.VMEM(lanes.shape, F32),
            pltpu.VMEM(side.shape, F32),
            pltpu.VMEM(bag_pick.shape, BF),
            pltpu.VMEM(bag_scale.shape, F32),
            pltpu.SemaphoreType.DMA((7,)),
        ],
    )
    got = exchanged(sent, 8)
    got_other = swapped(got)
    own_slots = slots // 2
    scaled, routed, gate_part, tower_part, table_part = call(
        own_kernel,
        shapes(
            ((own_slots, 2 * feature), BF),
            ((own_slots, feature), BF),
            ((2, feature), F32),
            ((2, feature), F32),
            (row_table.shape, F32),
        ),
        (received, got, tower_weight, row_table),
        1 << 29,
        "own",
        12,
    )
    table_tile = row_table.shape[0] // tiles
    in_grad, out_grad, gate_grad, tower_grad, new_table = call(
        final_kernel,
        shapes(
            ((half, feature), F32),
            ((half, feature), F32),
            ((2, feature), F32),
            ((2, feature), F32),
            (row_table.shape, F32),
        ),
        (
            received_other,
            got_other,
            scaled,
            routed,
            far(act_t),
            far(grad_t),
            slope,
            tower_weight,
            gate_part,
            tower_part,
            table_part,
        ),
        6 << 30,
        "final",
        40,
        grid=(tiles,),
        in_specs=[
            full(received.shape),
            full(got.shape),
            full(scaled.shape),
            full(routed.shape),
            in_hbm,
            in_hbm,
            pl.BlockSpec((tile, 128), lambda i: (i, 0)),
            full(tower_weight.shape),
            full((2, feature)),
            full((2, feature)),
            pl.BlockSpec((table_tile, feature), lambda i: (i, 0)),
        ],
        out_specs=[
            pl.BlockSpec((tile, feature), lambda i: (i, 0)),
            pl.BlockSpec((tile, feature), lambda i: (i, 0)),
            full((2, feature)),
            full((2, feature)),
            pl.BlockSpec((table_tile, feature), lambda i: (i, 0)),
        ],
        scratch_shapes=[
            pltpu.VMEM((own_slots, 2 * feature), BF),
            pltpu.VMEM((own_slots, feature), BF),
            pltpu.VMEM((8, tall), F32),
            pltpu.VMEM((half, slots), BF),
            pltpu.VMEM((half, slots), BF),
            pltpu.SemaphoreType.DMA((2, tiles)),
        ],
    )
    return (in_grad[None], out_grad[None], gate_grad[None], tower_grad, new_table)


def solution(mesh):
    split = Mesh(
        mesh.devices.reshape(4, 8, 4, mesh.shape["dp"]), ("expert_0", "expert_1", "expert_2", "dp")
    )
    in_specs = (
        P(EXPERT_DP, None),
        P(EXPERT_DP, None),
        P(EXPERT_DP, None),
        P(EXPERT, None, None),
        P(EXPERT, None, None),
        P(),
        P(),
        P(),
        P(EXPERT_DP),
        P(EXPERT_DP),
        P(EXPERT_DP),
        P(EXPERT, None),
    )
    out_specs = (
        P(EXPERT, "dp", None),
        P(EXPERT, "dp", None),
        P(EXPERT, None, None),
        P(),
        P(EXPERT, None),
    )
    return jax.shard_map(
        on_device, mesh=split, in_specs=in_specs, out_specs=out_specs, check_vma=False
    )
```

```python
import functools

import jax
import jax.numpy as jnp
from jax import lax
from jax.experimental import pallas as pl
from jax.experimental.pallas import tpu as pltpu
from jax.sharding import Mesh
from jax.sharding import PartitionSpec as P

EXPERT = ("expert_0", "expert_1", "expert_2")
EXPERT_DP = ("expert_0", "expert_1", "expert_2", "dp")

LOSS_SCALE = 32.0
STEP_SIZE = 0.25
BF = jnp.bfloat16
F32 = jnp.float32

ROWS = 2
BLOCKS = 3
PIECES = 3
SLOT_LANES = 4 * PIECES
SLOTS = ROWS * BLOCKS
ROW_LANES = SLOTS * SLOT_LANES
ENTRIES = 4
SIDE_ROW = 4
TOWER_ROW = 5


def dot(left, right):
    return jnp.dot(left, right, preferred_element_type=F32)


def dot_last(left, right):
    return lax.dot_general(left, right, (((1,), (1,)), ((), ())), preferred_element_type=F32)


def iota(shape, dim):
    return lax.broadcasted_iota(jnp.int32, shape, dim)


def ones_where(mask):
    return jnp.where(mask, 1.0, 0.0).astype(BF)


def three_pieces(value):
    high = value.astype(BF)
    rest = value - high.astype(F32)
    middle = rest.astype(BF)
    low = (rest - middle.astype(F32)).astype(BF)
    return high, middle, low


def tower_pieces(tower):
    pieces = three_pieces(tower)
    row = iota((8, tower.shape[1]), 0)
    stacked = jnp.zeros((8, tower.shape[1]), F32)
    for p, piece in enumerate(pieces):
        for t in range(2):
            stacked = jnp.where(row == 2 * p + t, piece[t : t + 1].astype(F32), stacked)
    return stacked.astype(BF)


def silu_and_slope(pre):
    sigma = 0.5 * jnp.tanh(0.5 * pre) + 0.5
    act = pre * sigma
    return act, sigma + act * (1.0 - sigma)


def full(shape):
    return pl.BlockSpec(shape, lambda *_: (0,) * len(shape))


def call(kernel, out_shape, ins, flops, name, mib, **more):
    return pl.pallas_call(
        kernel,
        out_shape=out_shape,
        cost_estimate=pl.CostEstimate(flops=flops, transcendentals=0, bytes_accessed=1 << 20),
        name=name,
        compiler_params=pltpu.CompilerParams(vmem_limit_bytes=mib << 20),
        **more,
    )(*ins)


def dispatch_kernel(routes_far, pooled_far, out, routes_t, pooled, sems):
    pairs = ((routes_far, routes_t), (pooled_far, pooled))
    copies = [pltpu.make_async_copy(far, near, sems.at[m]) for m, (far, near) in enumerate(pairs)]
    for copy in copies:
        copy.start()
    tok = pooled.shape[0]
    copies[0].wait()
    shape = (out.shape[0], tok)
    row = iota(shape, 0)
    owner = row >> 1
    named = (owner == routes_t[0:1, :]) | (owner == routes_t[1:2, :])
    earlier = ones_where(iota((tok, tok), 0) < iota((tok, tok), 1))
    rank = dot(ones_where(named), earlier)
    first = (BLOCKS * (row & 1)).astype(F32)
    feature = pooled.shape[1]
    copies[1].wait()
    for c in range(BLOCKS):
        pick = ones_where(named & (rank == first + c))
        out[:, c * feature : (c + 1) * feature] = dot(pick, pooled[...]).astype(BF)


def prepare_kernel(
    routes, routes_t, pooled, gate_flat, labels, bag_rows, bag_sample, bag_weight,
    take, put, gate_rows, lanes, side, bag_pick, bag_scale,
):
    tok = pooled.shape[0]
    rows = gate_flat.shape[0]
    owners = bag_rows.shape[0]
    row = iota((tok, rows), 1)
    named = [(row >> 1) == routes[:, k : k + 1] for k in range(2)]
    earlier = ones_where(iota((tok, tok), 0) > iota((tok, tok), 1))
    rank = dot(earlier, ones_where(named[0] | named[1]))
    first = (BLOCKS * (row & 1)).astype(F32)
    for k in range(2):
        for c in range(BLOCKS):
            take[k, :, c * rows : (c + 1) * rows] = ones_where(named[k] & (rank == first + c))
    owner = iota((owners, tok), 0)
    named_t = [owner == routes_t[k : k + 1, :] for k in range(2)]
    later = ones_where(iota((tok, tok), 0) < iota((tok, tok), 1))
    rank_t = dot(ones_where(named_t[0] | named_t[1]), later)
    for k in range(2):
        for j in range(SLOTS):
            put[SLOTS * k + j] = ones_where(named_t[k] & (rank_t == float(j)))
    logits = dot_last(pooled[...], gate_flat[...])
    lane = iota((tok, 128), 1)
    gate = jnp.zeros((tok, 128), F32)
    label = jnp.zeros((tok, 128), F32)
    for t in range(2):
        of_task = (row & 1) == t
        chosen = [
            jnp.sum(jnp.where(named[k] & of_task, logits, 0.0), axis=1, keepdims=True)
            for k in range(2)
        ]
        gate = jnp.where(lane == t, jax.nn.sigmoid(chosen[0] - chosen[1]), gate)
        label = jnp.where(lane == t, labels[:, t : t + 1].astype(F32), label)
        signs = jnp.where(named[0] & of_task, 1.0, jnp.where(named[1] & of_task, -1.0, 0.0))
        gate_rows[t] = dot(signs.astype(BF), gate_flat[...])
    lanes[0] = gate
    lanes[1] = label
    numbers = jnp.zeros((owners, 128), jnp.int32)
    side_lane = iota((owners, 128), 1)
    for r in range(ENTRIES):
        number = bag_rows[:, r : r + 1]
        numbers = jnp.where(side_lane == ROW_LANES + 2 * r, number >> 8, numbers)
        numbers = jnp.where(side_lane == ROW_LANES + 2 * r + 1, number & 255, numbers)
    side[...] = numbers.astype(F32)
    tall = bag_pick.shape[0]
    spread = ones_where((iota((tall, owners), 0) >> 3) == iota((tall, owners), 1))
    entry = iota((tall, ENTRIES), 0) & 7
    mine = entry == iota((tall, ENTRIES), 1)

    def column(value):
        spread_out = sum(dot(spread, piece) for piece in three_pieces(value))
        return jnp.sum(jnp.where(mine, spread_out, 0.0), axis=1, keepdims=True)

    sample = column(bag_sample[...].astype(F32))
    tall_iota = iota((tall, tok), 0) & 7
    hit = (sample == iota((tall, tok), 1).astype(F32)) & (tall_iota < ENTRIES)
    bag_pick[...] = ones_where(hit)
    bag_scale[...] = jnp.broadcast_to(column(bag_weight[...]), bag_scale.shape)


def slope_kernel(w_out, tower, slopes):
    found = dot_last(tower_pieces(tower[...]), w_out[...])
    for t in range(2):
        slopes[t : t + 1, :] = found[t : t + 1] + found[2 + t : 3 + t] + found[4 + t : 5 + t]


def expert_kernel(x, w_in, w_out, slopes, out, total, stacked):
    step = pl.program_id(0)
    rows = x.shape[0]
    feature = w_in.shape[1]
    wide = 3 * feature

    @pl.when(step == 0)
    def _():
        total[...] = jnp.zeros_like(total)
        for c in range(BLOCKS):
            stacked[c * rows : (c + 1) * rows, :] = x[:, c * feature : (c + 1) * feature]

    act, grad = silu_and_slope(dot_last(stacked[...], w_in[...]))
    total[:, :feature] += dot(act.astype(BF), w_out[...])
    for t in range(2):
        cols = slice((1 + t) * feature, (2 + t) * feature)
        total[:, cols] += dot((grad * slopes[t : t + 1, :]).astype(BF), w_in[...])

    @pl.when(step == pl.num_programs(0) - 1)
    def _():
        for c in range(BLOCKS):
            out[:, c * wide : (c + 1) * wide] = total[c * rows : (c + 1) * rows, :].astype(BF)


def half_kernel(half, x, x_other, w_in, w_out, tower, act_t, grad_t, slope):
    del half
    feature = w_in.shape[1]
    rows = x.shape[0]
    slopes = dot_last(w_out[...], tower_pieces(tower[...]))
    lane = iota(slope.shape, 1)
    wide = jnp.zeros(slope.shape, F32)
    for t in range(2):
        column = slopes[:, t : t + 1] + slopes[:, 2 + t : 3 + t] + slopes[:, 4 + t : 5 + t]
        wide = jnp.where(lane == t, column, wide)
    slope[...] = wide
    for r, source in enumerate((x, x_other)):
        for c in range(BLOCKS):
            pre = dot_last(w_in[...], source[:, c * feature : (c + 1) * feature])
            act, grad = silu_and_slope(pre)
            at = (BLOCKS * r + c) * rows
            act_t[:, at : at + rows] = act.astype(BF)
            grad_t[:, at : at + rows] = grad.astype(BF)


def sample_kernel(
    back, take_far, put_far, gate_rows_far, lanes_far, side_far, bag_pick_far, bag_scale_far,
    tower, bias, after,
    out, take, put, gate_rows, lanes, side, bag_pick, bag_scale, stacked, sems,
):
    del after
    pairs = (
        (take_far, take),
        (lanes_far, lanes),
        (gate_rows_far, gate_rows),
        (bag_pick_far, bag_pick),
        (bag_scale_far, bag_scale),
        (put_far, put),
        (side_far, side),
    )
    copies = [pltpu.make_async_copy(far, near, sems.at[m]) for m, (far, near) in enumerate(pairs)]
    for copy in copies:
        copy.start()
    feature = tower.shape[1]
    wide = 3 * feature
    rows = back.shape[0]
    for c in range(BLOCKS):
        stacked[c * rows : (c + 1) * rows, :] = back[:, c * wide : (c + 1) * wide]
    copies[0].wait()
    parts = [dot(take[k], stacked[...]) for k in range(2)]
    task_row = iota((128, feature), 0)
    weights = [
        jnp.where(task_row == 0, piece[0:1].astype(F32), jnp.where(task_row == 1, piece[1:2].astype(F32), 0.0)).astype(BF)
        for piece in three_pieces(tower[...])
    ]
    along = []
    for k in range(2):
        result = parts[k][:, :feature].astype(BF)
        along.append(sum(dot_last(result, weight) for weight in weights))
    for copy in copies[1:]:
        copy.wait()
    first, label = lanes[0], lanes[1]
    second = 1.0 - first
    lane = iota(first.shape, 1)
    lane_bias = jnp.where(lane == 0, bias[0], bias[1])
    logit = first * along[0] + second * along[1] + lane_bias
    logit_grad = jnp.where(lane < 2, LOSS_SCALE * (jax.nn.sigmoid(logit) - label), 0.0)
    pulls = [first * logit_grad, second * logit_grad]
    first_grad = logit_grad * (along[0] - along[1]) * first * second
    pooled_grad = first_grad[:, 0:1] * gate_rows[0] + first_grad[:, 1:2] * gate_rows[1]
    towers = [0.0, 0.0]
    for k in range(2):
        for t in range(2):
            pull = jnp.broadcast_to(pulls[k][:, t : t + 1], (first.shape[0], feature))
            pooled_grad += pull * parts[k][:, (1 + t) * feature : (2 + t) * feature]
            towers[t] += jnp.sum(pull * parts[k][:, :feature], axis=0, keepdims=True)
    picked = sum(dot(bag_pick[...], piece) for piece in three_pieces(pooled_grad))
    placed = [None] * SLOTS
    for k in range(2):
        signed = first_grad if k == 0 else -first_grad
        packed = 0.0
        for kind, value in enumerate((pulls[k], signed)):
            for p, piece in enumerate(three_pieces(value)):
                piece = piece.astype(F32)
                shift = 2 * PIECES * kind + 2 * p
                packed += pltpu.roll(piece, shift, 1) if shift else piece
        packed = packed.astype(BF)
        for j in range(SLOTS):
            part = dot(put[SLOTS * k + j], packed)
            placed[j] = part if k == 0 else placed[j] + part
    extra = side[...] + placed[0]
    for j in range(1, SLOTS):
        extra += pltpu.roll(placed[j], j * SLOT_LANES, 1)
    tall, owners = bag_pick.shape[0], side.shape[0]
    spread = ones_where(iota((tall, owners), 0) == 8 * iota((tall, owners), 1) + SIDE_ROW)
    extra = dot(spread, extra.astype(BF))
    which = iota((tall, 128), 0) & 7
    for at in range(0, feature, 128):
        cols = slice(at, at + 128)
        value = bag_scale[...] * picked[:, cols]
        for t in range(2):
            value = jnp.where(which == TOWER_ROW + t, towers[t][:, cols], value)
        out[:, cols] = (value + extra if at == 0 else value).astype(BF)


def decode(inputs, source, tower, scaled, routed):
    feature = tower.shape[1]
    rows, tall = inputs.shape[0], source.shape[0]
    row = iota((rows, tall), 0)
    expand = ones_where(iota((rows, tall), 1) == 8 * (row >> 1) + SIDE_ROW)
    lane = iota((rows, 128), 1)
    half_lanes = BLOCKS * SLOT_LANES
    odd = (iota((rows, 128), 0) & 1) == 1
    own = (odd & (lane >= half_lanes) & (lane < ROW_LANES)) | (~odd & (lane < half_lanes))
    source_lane = iota((128, feature), 0)
    within = jnp.where(source_lane >= half_lanes, source_lane - half_lanes, source_lane)
    side = jnp.where(own, dot(expand, source[:, :128]), 0.0).astype(BF)
    gate_total = [jnp.zeros((1, feature), F32) for _ in range(2)]
    for c in range(BLOCKS):
        values = []
        for v in range(4):
            base = c * SLOT_LANES + 2 * PIECES * (v // 2) + v % 2
            values.append(dot(side, ones_where((within == base) | (within == base + 2) | (within == base + 4))))
        block = inputs[:, c * feature : (c + 1) * feature].astype(F32)
        at = slice(c * rows, (c + 1) * rows)
        routed[at, :] = (values[0] * tower[0:1, :] + values[1] * tower[1:2, :]).astype(BF)
        for t in range(2):
            scaled[at, t * feature : (t + 1) * feature] = (values[t] * block).astype(BF)
            gate_total[t] += jnp.sum(values[2 + t] * block, axis=0, keepdims=True)
    tower_pick = ones_where((iota((8, tall), 1) & 7) == TOWER_ROW + iota((8, tall), 0))
    tower_total = dot(tower_pick, source[...])
    wanted, asked = iota((8, 128), 1), iota((8, 128), 0)
    select = jnp.where(wanted == ROW_LANES + 2 * asked, 256.0, 0.0)
    select = jnp.where(wanted == ROW_LANES + 2 * asked + 1, 1.0, select).astype(BF)
    numbers = dot_last(select, source[:, :128])
    which = iota((1, tall), 1) & 7
    target = jnp.full((1, tall), -1.0, F32)
    for e in range(ENTRIES):
        moved = pltpu.roll(numbers, tall + e - SIDE_ROW, 1)
        target = jnp.where(which == e, moved[e : e + 1], target)
    return gate_total, tower_total, target


def row_sums(target, source, start, depth):
    number = (start + iota((depth, source.shape[0]), 0)).astype(F32)
    return dot(ones_where(number == target), source[...])


def own_kernel(x, got, tower, table, scaled, routed, gate_part, tower_part, table_part):
    gate_total, tower_total, target = decode(x, got, tower, scaled, routed)
    for t in range(2):
        gate_part[t : t + 1, :] = gate_total[t]
        tower_part[t : t + 1, :] = tower_total[t : t + 1]
    depth = 256
    for start in range(0, table.shape[0], depth):
        at = slice(start, start + depth)
        table_part[at, :] = table[at, :] - STEP_SIZE * row_sums(target, got, start, depth)


def final_kernel(
    x_other, got_other, scaled_own, routed_own, act_far, grad_far, slope, tower,
    gate_part, tower_part, table_part,
    in_grad, out_grad, gate_grad, tower_grad, new_table,
    scaled, routed, targets, act_t, grad_t, sems,
):
    feature = tower.shape[1]
    step = pl.program_id(0)
    tile = in_grad.shape[0]

    def arriving(n):
        part = pl.ds(n * tile, tile)
        pairs = ((grad_far, grad_t), (act_far, act_t))
        return [
            pltpu.make_async_copy(distant.at[part, :], near.at[part, :], sems.at[m, n])
            for m, (distant, near) in enumerate(pairs)
        ]

    @pl.when(step == 0)
    def _():
        for n in range(act_t.shape[0] // tile):
            for copy in arriving(n):
                copy.start()
        gate_total, tower_total, target = decode(x_other, got_other, tower, scaled, routed)
        targets[...] = jnp.broadcast_to(target, targets.shape)
        for t in range(2):
            gate_grad[t : t + 1, :] = gate_part[t : t + 1, :] + gate_total[t]
            tower_grad[t : t + 1, :] = tower_part[t : t + 1, :] + tower_total[t : t + 1]

    for copy in arriving(step):
        copy.wait()
    part = pl.ds(pl.multiple_of(step * tile, tile), tile)
    split = scaled.shape[0]
    both = dot(grad_t[part, :split], scaled_own[...]) + dot(grad_t[part, split:], scaled[...])
    in_grad[...] = slope[:, 0:1] * both[:, :feature] + slope[:, 1:2] * both[:, feature:]
    out_grad[...] = dot(act_t[part, :split], routed_own[...]) + dot(act_t[part, split:], routed[...])
    depth = new_table.shape[0]
    sums = row_sums(targets[0:1, :], got_other, step * depth, depth)
    new_table[...] = table_part[...] - STEP_SIZE * sums


def exchanged(rows, each):
    width = rows.shape[1]
    moved = lax.all_to_all(rows.reshape(-1, each, width), EXPERT, split_axis=0, concat_axis=0, tiled=True)
    return moved.reshape(-1, width)


def swapped(shard):
    return lax.ppermute(shard, "dp", [(0, 1), (1, 0)])


def far(array):
    return pltpu.with_memory_space_constraint(array, pltpu.HBM)


def shapes(*items):
    return tuple(jax.ShapeDtypeStruct(shape, dtype) for shape, dtype in items)


def on_device(
    pooled,
    routes,
    labels,
    in_weight,
    out_weight,
    gate_weight,
    tower_weight,
    tower_bias,
    bag_rows,
    bag_sample,
    bag_weight,
    row_table,
):
    owners = lax.axis_size(EXPERT)
    tok, feature = pooled.shape
    hidden = in_weight.shape[1]
    half = hidden // lax.axis_size("dp")
    rows = ROWS * owners
    slots = 2 * BLOCKS * rows
    in_matrix, out_matrix = in_weight[0], out_weight[0]
    gate_flat = gate_weight.reshape(-1, feature)
    routes_t = routes.T
    in_vmem = pl.BlockSpec(memory_space=pltpu.VMEM)
    in_hbm = pl.BlockSpec(memory_space=pltpu.HBM)
    outbound = call(
        dispatch_kernel,
        jax.ShapeDtypeStruct((rows, BLOCKS * feature), BF),
        (far(routes_t), far(pooled)),
        1 << 27,
        "dispatch",
        4,
        in_specs=[in_hbm, in_hbm],
        out_specs=in_vmem,
        scratch_shapes=[
            pltpu.VMEM(routes_t.shape, jnp.int32),
            pltpu.VMEM(pooled.shape, BF),
            pltpu.SemaphoreType.DMA((2,)),
        ],
    )
    received = exchanged(outbound, ROWS)
    tall = 8 * owners
    take, put, gate_rows, lanes, side, bag_pick, bag_scale = call(
        prepare_kernel,
        shapes(
            ((2, tok, BLOCKS * rows), BF),
            ((2 * SLOTS, owners, tok), BF),
            ((2, tok, feature), F32),
            ((2, tok, 128), F32),
            ((owners, 128), F32),
            ((tall, tok), BF),
            ((tall, 128), F32),
        ),
        (
            routes,
            routes_t,
            pooled,
            gate_flat,
            labels,
            bag_rows.reshape(owners, ENTRIES),
            bag_sample.reshape(owners, ENTRIES),
            bag_weight.reshape(owners, ENTRIES),
        ),
        1 << 31,
        "prepare",
        60,
    )
    depth = hidden // 2
    slopes = call(
        slope_kernel,
        jax.ShapeDtypeStruct((2, hidden), F32),
        (out_matrix, tower_weight),
        1 << 31,
        "slopes",
        12,
        grid=(hidden // depth,),
        in_specs=[pl.BlockSpec((depth, feature), lambda i: (i, 0)), full(tower_weight.shape)],
        out_specs=pl.BlockSpec((2, depth), lambda i: (0, i)),
    )
    piece = hidden // 2
    message = call(
        expert_kernel,
        jax.ShapeDtypeStruct((rows, 3 * BLOCKS * feature), BF),
        (received, far(in_matrix), far(out_matrix), slopes),
        7 << 30,
        "expert",
        32,
        grid=(hidden // piece,),
        in_specs=[
            full(received.shape),
            pl.BlockSpec((piece, feature), lambda i: (i, 0)),
            pl.BlockSpec((piece, feature), lambda i: (i, 0)),
            pl.BlockSpec((2, piece), lambda i: (0, i)),
        ],
        out_specs=full((rows, 3 * BLOCKS * feature)),
        scratch_shapes=[
            pltpu.VMEM((BLOCKS * rows, 3 * feature), F32),
            pltpu.VMEM((BLOCKS * rows, feature), BF),
        ],
    )
    returned = exchanged(message, ROWS)
    received_other = swapped(received)
    tile = 512
    tiles = half // tile
    which = jnp.full((1,), lax.axis_index("dp"), jnp.int32)
    act_t, grad_t, slope = call(
        half_kernel,
        shapes(((half, slots), BF), ((half, slots), BF), ((half, 128), F32)),
        (which, received, received_other, in_matrix, out_matrix, tower_weight),
        7 << 30,
        "half",
        56,
        grid_spec=pltpu.PrefetchScalarGridSpec(
            num_scalar_prefetch=1,
            grid=(tiles,),
            in_specs=[
                full(received.shape),
                full(received.shape),
                pl.BlockSpec((tile, feature), lambda i, part: (part[0] * tiles + i, 0)),
                pl.BlockSpec((tile, feature), lambda i, part: (part[0] * tiles + i, 0)),
                full(tower_weight.shape),
            ],
            out_specs=[
                pl.BlockSpec((tile, slots), lambda i, part: (i, 0)),
                pl.BlockSpec((tile, slots), lambda i, part: (i, 0)),
                pl.BlockSpec((tile, 128), lambda i, part: (i, 0)),
            ],
        ),
    )
    sent = call(
        sample_kernel,
        jax.ShapeDtypeStruct((tall, feature), BF),
        (
            returned,
            far(take),
            far(put),
            far(gate_rows),
            far(lanes),
            far(side),
            far(bag_pick),
            far(bag_scale),
            tower_weight,
            tower_bias,
            far(slope),
        ),
        1 << 29,
        "sample",
        16,
        in_specs=[in_vmem] + [in_hbm] * 7 + [in_vmem]
        + [pl.BlockSpec(memory_space=pltpu.SMEM), pl.BlockSpec(memory_space=pl.ANY)],
        out_specs=in_vmem,
        scratch_shapes=[
            pltpu.VMEM(take.shape, BF),
            pltpu.VMEM(put.shape, BF),
            pltpu.VMEM(gate_rows.shape, F32),
            pltpu.VMEM(lanes.shape, F32),
            pltpu.VMEM(side.shape, F32),
            pltpu.VMEM(bag_pick.shape, BF),
            pltpu.VMEM(bag_scale.shape, F32),
            pltpu.VMEM((BLOCKS * rows, 3 * feature), BF),
            pltpu.SemaphoreType.DMA((7,)),
        ],
    )
    got = exchanged(sent, 8)
    got_other = swapped(got)
    own_slots = slots // 2
    scaled, routed, gate_part, tower_part, table_part = call(
        own_kernel,
        shapes(
            ((own_slots, 2 * feature), BF),
            ((own_slots, feature), BF),
            ((2, feature), F32),
            ((2, feature), F32),
            (row_table.shape, F32),
        ),
        (received, got, tower_weight, row_table),
        1 << 29,
        "own",
        12,
    )
    table_tile = row_table.shape[0] // tiles
    in_grad, out_grad, gate_grad, tower_grad, new_table = call(
        final_kernel,
        shapes(
            ((half, feature), F32),
            ((half, feature), F32),
            ((2, feature), F32),
            ((2, feature), F32),
            (row_table.shape, F32),
        ),
        (
            received_other,
            got_other,
            scaled,
            routed,
            far(act_t),
            far(grad_t),
            slope,
            tower_weight,
            gate_part,
            tower_part,
            table_part,
        ),
        6 << 30,
        "final",
        40,
        grid=(tiles,),
        in_specs=[
            full(received.shape),
            full(got.shape),
            full(scaled.shape),
            full(routed.shape),
            in_hbm,
            in_hbm,
            pl.BlockSpec((tile, 128), lambda i: (i, 0)),
            full(tower_weight.shape),
            full((2, feature)),
            full((2, feature)),
            pl.BlockSpec((table_tile, feature), lambda i: (i, 0)),
        ],
        out_specs=[
            pl.BlockSpec((tile, feature), lambda i: (i, 0)),
            pl.BlockSpec((tile, feature), lambda i: (i, 0)),
            full((2, feature)),
            full((2, feature)),
            pl.BlockSpec((table_tile, feature), lambda i: (i, 0)),
        ],
        scratch_shapes=[
            pltpu.VMEM((own_slots, 2 * feature), BF),
            pltpu.VMEM((own_slots, feature), BF),
            pltpu.VMEM((8, tall), F32),
            pltpu.VMEM((half, slots), BF),
            pltpu.VMEM((half, slots), BF),
            pltpu.SemaphoreType.DMA((2, tiles)),
        ],
    )
    return (in_grad[None], out_grad[None], gate_grad[None], tower_grad, new_table)


def solution(mesh):
    split = Mesh(
        mesh.devices.reshape(4, 8, 4, mesh.shape["dp"]), ("expert_0", "expert_1", "expert_2", "dp")
    )
    in_specs = (
        P(EXPERT_DP, None),
        P(EXPERT_DP, None),
        P(EXPERT_DP, None),
        P(EXPERT, None, None),
        P(EXPERT, None, None),
        P(),
        P(),
        P(),
        P(EXPERT_DP),
        P(EXPERT_DP),
        P(EXPERT_DP),
        P(EXPERT, None),
    )
    out_specs = (
        P(EXPERT, "dp", None),
        P(EXPERT, "dp", None),
        P(EXPERT, None, None),
        P(),
        P(EXPERT, None),
    )
    return jax.shard_map(
        on_device, mesh=split, in_specs=in_specs, out_specs=out_specs, check_vma=False
    )
```
